32 devices in a mesh: tensor: 4 (over z), group: 4 (over y, core), cross: 2 (over x).
Axes of the slice: x: 2, y: 2, z: 4, core: 2. Of those that a mesh axis runs over, the one named last changes fastest.
Arguments:
- inputs: bfloat16 [16, 1568, 1024], P(('group', 'cross'), 'tensor'), may hold values from -6 to 6
- clips_here: int32 [8], P(('group', 'cross')), may hold values from 1 to 2, as said below
- first_gain: bfloat16 [1024], replicated, may hold values from 0.5 to 1.5
- first_shift: bfloat16 [1024], replicated, may hold values from -1.25 to 1.25
- query_key_value: bfloat16 [3, 1024, 1024], P(None, 'group', 'tensor'), may hold values from -0.1875 to 0.1875
- query_bias: bfloat16 [1024], P('tensor'), may hold values from -3 to 3
- value_bias: bfloat16 [1024], P('tensor'), may hold values from -0.1875 to 0.1875
- output_weight: bfloat16 [1024, 1024], P('tensor', 'group'), may hold values from -6 to 6
- output_bias: bfloat16 [1024], replicated, may hold values from -3 to 3
- second_gain: bfloat16 [1024], replicated, may hold values from 0.5 to 1.5
- second_shift: bfloat16 [1024], replicated, may hold values from -1.25 to 1.25
- expand_weight: bfloat16 [1024, 4096], P('group', 'tensor'), may hold values from -0.1875 to 0.1875
- expand_bias: bfloat16 [4096], P('tensor'), may hold values from -3 to 3
- contract_weight: bfloat16 [4096, 1024], P('tensor', 'group'), may hold values from -0.09375 to 0.09375
- contract_bias: bfloat16 [1024], replicated, may hold values from -3 to 3
- output_grad: bfloat16 [16, 1568, 1024], P(('group', 'cross'), 'tensor'), may hold values from -6 to 6
Outputs:
- output: bfloat16 [16, 1568, 1024], P(('group', 'cross'), 'tensor')
- input_grad: bfloat16 [16, 1568, 1024], P(('group', 'cross'), 'tensor')
- first_gain_grad: float32 [1024], P('group')
- first_shift_grad: float32 [1024], P('group')
- query_key_value_grad: float32 [3, 1024, 1024], P(None, 'group', 'tensor')
- query_bias_grad: float32 [1024], P(('tensor', 'group'))
- value_bias_grad: float32 [1024], P(('tensor', 'group'))
- output_weight_grad: float32 [1024, 1024], P('tensor', 'group')
- output_bias_grad: float32 [1024], P('group')
- second_gain_grad: float32 [1024], P('group')
- second_shift_grad: float32 [1024], P('group')
- expand_weight_grad: float32 [1024, 4096], P('group', 'tensor')
- expand_bias_grad: float32 [4096], P(('tensor', 'group'))
- contract_weight_grad: float32 [4096, 1024], P('tensor', 'group')
- contract_bias_grad: float32 [1024], P('group')
The draws below stay inside these ranges and needn't reach their ends.
Inputs may be any that keep to these rules, and one draw needn't show every extreme that they name: Exactly half of the 8 data positions hold 2 clips and the others 1; slot p * 2 + j holds a clip if j < clips_here[p].
All inputs are finite; a program needn't handle non-finite values.
Results may differ from the reference program's by a relative error of at most 0.02.
Values may be sent and summed in bfloat16 or wider, within the bound.
A program may use at most 192 MiB of HBM per device.

```python
import jax
import jax.numpy as jnp
from jax import lax

D = 1024
HEADS = 16
HEAD = 64
FF = 4096
CLIP = 1568
SLOTS = 2
POS = 8
ALLSLOTS = 16


def draw_clips_here(key, part):
    order = jax.random.permutation(key, POS)
    return (1 + (order < POS // 2)).astype(jnp.int32)


def levels(own_key, extent, shards, least, high):
    def one(position, blocks):
        heights = jax.random.uniform(jax.random.fold_in(jax.random.fold_in(own_key, 6), position), (blocks,), jnp.float32, least / len(shards), high / len(shards))
        return jnp.repeat(jnp.exp(heights), extent[position] // blocks).reshape((-1,) + (1,) * (len(extent) - position - 1))

    loudness = one(*shards[0])
    for cut in shards[1:]:
        loudness = loudness * one(*cut)
    return loudness


def noise(key, shape, deviation, limit, pieces=(), held_as=jnp.bfloat16):
    values = jax.random.normal(key, shape, jnp.float32) * deviation
    if len(pieces) > 0:
        values = levels(key, shape, pieces, -0.22, 0.18) * values
    return jnp.clip(values, min=-limit, max=limit).astype(held_as)


def setup_inputs(seed: int = 0) -> dict:
    splits = jax.random.split(jax.random.key(seed), 17)
    inputs = noise(splits[0], (ALLSLOTS, CLIP, D), 1.0, 6.0, ((0, 8), (1, 4)))
    clips_here = draw_clips_here(jax.random.fold_in(splits[16], 71), 0)
    first_gain = jnp.clip(1.0 + 0.1 * jax.random.normal(splits[2], (D,), jnp.float32), 0.5, 1.5).astype(jnp.bfloat16)
    first_shift = noise(splits[3], (D,), 0.2, 1.25)
    query_key_value = noise(splits[4], (3, D, D), D ** -0.5, 0.1875, ((1, 4), (2, 4)))
    query_bias = noise(splits[5], (D,), 0.5, 3.0, ((0, 4),))
    value_bias = noise(splits[6], (D,), 0.03, 0.1875, ((0, 4),))
    output_weight = noise(splits[7], (D, D), (max(1, D // CLIP)) ** -0.5, 6.0, ((0, 4), (1, 4)))
    output_bias = noise(splits[8], (D,), 0.5, 3.0)
    second_gain = jnp.clip(1.0 + 0.1 * jax.random.normal(splits[9], (D,), jnp.float32), 0.5, 1.5).astype(jnp.bfloat16)
    second_shift = noise(splits[10], (D,), 0.2, 1.25)
    expand_weight = noise(splits[11], (D, FF), D ** -0.5, 0.1875, ((0, 4), (1, 4)))
    expand_bias = noise(splits[12], (FF,), 0.5, 3.0, ((0, 4),))
    contract_weight = noise(splits[13], (FF, D), FF ** -0.5, 0.09375, ((0, 4), (1, 4)))
    contract_bias = noise(splits[14], (D,), 0.5, 3.0)
    output_grad = noise(splits[15], (ALLSLOTS, CLIP, D), 1.0, 6.0, ((0, 8), (1, 4)))
    return {"inputs": inputs, "clips_here": clips_here, "first_gain": first_gain, "first_shift": first_shift, "query_key_value": query_key_value, "query_bias": query_bias, "value_bias": value_bias, "output_weight": output_weight, "output_bias": output_bias, "second_gain": second_gain, "second_shift": second_shift, "expand_weight": expand_weight, "expand_bias": expand_bias, "contract_weight": contract_weight, "contract_bias": contract_bias, "output_grad": output_grad}


@jax.custom_vjp
def low(v):
    return lax.optimization_barrier(v.astype(jnp.bfloat16)).astype(jnp.float32)

@jax.custom_vjp
def low_back(v):
    return v

def low_keep(v):
    return (low(v), None)

def low_pass(kept, grad):
    return (grad,)

def back_keep(v):
    return (v, None)

def back_low(kept, grad):
    return (low(grad),)
low.defvjp(low_keep, low_pass)
low_back.defvjp(back_keep, back_low)
epsilon = 1e-06
highest = lax.Precision.HIGHEST

def rounded_both(values):
    return low(low_back(values))

def layer_norm(values, norm_gain, norm_shift):
    center = values - lax.optimization_barrier(jnp.mean(values, axis=-1, keepdims=True))
    spread = lax.optimization_barrier(jnp.mean(center * center, axis=-1, keepdims=True))
    return center * lax.rsqrt(spread + epsilon) * norm_gain + norm_shift

def attend(query_rows, key_rows, value_rows):
    length = query_rows.shape[0]
    query_heads = query_rows.reshape(2, length // 2, HEADS, HEAD)
    key_heads = key_rows.reshape(length, HEADS, HEAD)
    value_heads = value_rows.reshape(length, HEADS, HEAD)

    def one_part(query_part):
        logits = low_back(jnp.einsum('bhe,lhe->hbl', query_part, key_heads, precision=highest))
        probs = jax.nn.softmax(logits * HEAD ** (-0.5), axis=-1)
        return jnp.einsum('hbl,lhe->bhe', low(probs), value_heads, precision=highest)
    attention_result = lax.map(jax.checkpoint(one_part), query_heads)
    return attention_result.reshape(length, HEADS * HEAD)

def block_forward(params, tokens):
    first_gain, first_shift, query_key_value, query_bias, value_bias, output_weight, output_bias, second_gain, second_shift, expand_weight, expand_bias, contract_weight, contract_bias = params
    first_normed = low(layer_norm(tokens, first_gain, first_shift))
    query_rows = rounded_both(jnp.dot(first_normed, query_key_value[0], precision=highest) + query_bias)
    key_rows = rounded_both(jnp.dot(first_normed, query_key_value[1], precision=highest))
    value_rows = rounded_both(jnp.dot(first_normed, query_key_value[2], precision=highest) + value_bias)
    attention_result = rounded_both(attend(query_rows, key_rows, value_rows))
    middle = tokens + low_back(jnp.dot(attention_result, output_weight, precision=highest) + output_bias)
    second_normed = low(layer_norm(middle, second_gain, second_shift))
    hidden_pre = low_back(jnp.dot(second_normed, expand_weight, precision=highest) + expand_bias)
    hidden_activation = low(jax.nn.gelu(hidden_pre, approximate=False))
    return middle + low_back(jnp.dot(hidden_activation, contract_weight, precision=highest) + contract_bias)

def reference(inputs, clips_here, first_gain, first_shift, query_key_value, query_bias, value_bias, output_weight, output_bias, second_gain, second_shift, expand_weight, expand_bias, contract_weight, contract_bias, output_grad):
    params = tuple((array_in.astype(jnp.float32) for array_in in (first_gain, first_shift, query_key_value, query_bias, value_bias, output_weight, output_bias, second_gain, second_shift, expand_weight, expand_bias, contract_weight, contract_bias)))
    slot_ids = jnp.arange(SLOTS * POS, dtype=jnp.int32)
    alive_mask = (slot_ids % SLOTS < clips_here[slot_ids // SLOTS]).astype(jnp.float32)

    def one_clip(totals, entries):
        tokens, cotangent, living = entries
        result, pullback = jax.vjp(block_forward, params, tokens.astype(jnp.float32))
        param_grads, token_grad = pullback(cotangent.astype(jnp.float32) * living)
        totals = jax.tree.map(jnp.add, totals, param_grads)
        return (totals, (result.astype(jnp.bfloat16), token_grad.astype(jnp.bfloat16)))
    zero_grads = tuple((jnp.zeros_like(array_in) for array_in in params))
    totals, (output, input_grad) = lax.scan(one_clip, zero_grads, (inputs, output_grad, alive_mask))
    return (output, input_grad, totals[0], totals[1], totals[2], totals[3], totals[4], totals[5], totals[6], totals[7], totals[8], totals[9], totals[10], totals[11], totals[12])
```

```python
import functools

import jax
import jax.numpy as jnp
from jax import lax
from jax.experimental import pallas as pl
from jax.experimental.pallas import tpu as pltpu
from jax.sharding import PartitionSpec as P

HEAD = 64
LANES = 128

epsilon = 1e-06
root_half = 0.7071067811865476
inv_root_two_pi = 0.3989422804014327
log_two = 0.6931471805599453
query_scale = HEAD**-0.5 / log_two

f32 = jnp.float32
bf16 = jnp.bfloat16

NN = (((1,), (0,)), ((), ()))
NT = (((1,), (1,)), ((), ()))
TN = (((0,), (0,)), ((), ()))


def dot(a, b, dims=NN):
    return lax.dot_general(a, b, dims, preferred_element_type=f32)


def attend_forward_kernel(q_ref, ka, kb, va, vb, o_ref, lse_ref, keys, values_low, values_high):
    n = ka.shape[0]

    @pl.when(pl.program_id(1) == 0)
    def _():
        low = lax.broadcasted_iota(jnp.int32, (n, LANES), 1) < HEAD
        one = jnp.ones((n, LANES), bf16)
        for i, (k, v) in enumerate(((ka, va), (kb, vb))):
            rows = slice(i * n, (i + 1) * n)
            keys[rows] = k[...]
            values_low[rows] = jnp.where(low, v[...], one)
            values_high[rows] = jnp.where(low, one, v[...])

    q = q_ref[...]
    low = lax.broadcasted_iota(jnp.int32, q.shape, 1) < HEAD
    zero = jnp.zeros_like(q)
    sums, tops = [], []
    for mine, v in ((jnp.where(low, q, zero), values_low), (jnp.where(low, zero, q), values_high)):
        s = dot(mine, keys[...], NT)
        top = jnp.max(s, axis=1, keepdims=True)
        p = jnp.exp2(s - top).astype(bf16)
        sums.append(dot(p, v[...]))
        tops.append(top)
    total = pltpu.roll(jnp.where(low, sums[1], sums[0]), HEAD, 1)
    o_ref[...] = (jnp.where(low, sums[0], sums[1]) / total).astype(bf16)
    lse_ref[...] = jnp.where(low, tops[0], tops[1]) + jnp.log2(total)


def attend_backward_kernel(
    q_ref, g_ref, o_ref, lse_ref, ka, kb, va, vb,
    dq_ref, dka, dkb, dva, dvb,
    keys, values, dk, dv,
):
    n = ka.shape[0]
    step = pl.program_id(1)

    @pl.when(step == 0)
    def _():
        for i, (k, v) in enumerate(((ka, va), (kb, vb))):
            keys[i * n : (i + 1) * n] = k[...]
            values[i * n : (i + 1) * n] = v[...]
        dk[...] = jnp.zeros_like(dk)
        dv[...] = jnp.zeros_like(dv)

    q, g = q_ref[...], g_ref[...]
    low = lax.broadcasted_iota(jnp.int32, q.shape, 1) < HEAD
    product = g.astype(f32) * o_ref[...].astype(f32)
    lse = lse_ref[...]
    q_t, g_t = q.T, g.T
    dqs = []
    for h in range(2):

        def own(a):
            zero = jnp.zeros_like(a)
            return jnp.where(low, a, zero) if h == 0 else jnp.where(low, zero, a)

        inner = jnp.sum(own(product), axis=1, keepdims=True)
        p = jnp.exp2(dot(own(q), keys[...], NT) - lse[:, HEAD * h : HEAD * h + 1])
        ds = (p * (dot(own(g), values[...], NT) - inner)).astype(bf16)
        dqs.append(dot(ds, keys[...]))
        rows = slice(HEAD * h, HEAD * (h + 1))
        dv[rows] += dot(g_t[rows], p.astype(bf16))
        dk[rows] += dot(q_t[rows], ds)
    dq_ref[...] = (jnp.where(low, dqs[0], dqs[1]) * HEAD**-0.5).astype(bf16)

    @pl.when(step == pl.num_programs(1) - 1)
    def _():
        key_total, value_total = (dk[...] * log_two).T, dv[...].T
        dka[...] = key_total[:n].astype(bf16)
        dkb[...] = key_total[n:].astype(bf16)
        dva[...] = value_total[:n].astype(bf16)
        dvb[...] = value_total[n:].astype(bf16)


def attend_forward(q, ka, kb, va, vb):
    n, width = q.shape
    spec = pl.BlockSpec((n, LANES), lambda i, j: (0, i))
    return pl.pallas_call(
        attend_forward_kernel,
        grid=(width // LANES, 1),
        in_specs=[spec] * 5,
        out_specs=[spec] * 2,
        out_shape=[jax.ShapeDtypeStruct((n, width), bf16), jax.ShapeDtypeStruct((n, width), f32)],
        scratch_shapes=[pltpu.VMEM((2 * n, LANES), bf16)] * 3,
        name="attend_forward",
        cost_estimate=pl.CostEstimate(
            flops=8 * n * n * width, bytes_accessed=16 * n * width, transcendentals=n * n * width // 32
        ),
        compiler_params=pltpu.CompilerParams(vmem_limit_bytes=56 << 20),
    )(q, ka, kb, va, vb)


def attend_backward(q, g, o, lse, ka, kb, va, vb):
    n, width = q.shape
    spec = pl.BlockSpec((n, LANES), lambda i, j: (0, i))
    return pl.pallas_call(
        attend_backward_kernel,
        grid=(width // LANES, 1),
        in_specs=[spec] * 8,
        out_specs=[spec] * 5,
        out_shape=[jax.ShapeDtypeStruct((n, width), bf16)] * 5,
        scratch_shapes=[pltpu.VMEM((2 * n, LANES), bf16)] * 2 + [pltpu.VMEM((LANES, 2 * n), f32)] * 2,
        name="attend_backward",
        cost_estimate=pl.CostEstimate(
            flops=20 * n * n * width, bytes_accessed=28 * n * width, transcendentals=n * n * width // 32
        ),
        compiler_params=pltpu.CompilerParams(vmem_limit_bytes=60 << 20),
    )(q, g, o, lse, ka, kb, va, vb)


def normalize(values):
    center = values - jnp.mean(values, axis=-1, keepdims=True)
    inverse = lax.rsqrt(jnp.mean(center * center, axis=-1, keepdims=True) + epsilon)
    return (center * inverse, inverse)


def normalize_back(upstream, normed, inverse, norm_gain):
    scaled = upstream * norm_gain
    return inverse * (
        scaled
        - jnp.mean(scaled, axis=-1, keepdims=True)
        - normed * jnp.mean(scaled * normed, axis=-1, keepdims=True)
    )


def clip_exchange(tensor_count, group_count):
    there, back = [], []
    for turn in range(2):
        pairs = []
        for z in range(tensor_count):
            for g in range(group_count):
                slot = (turn + z) % 2
                target = (2 * slot + g % 2) * group_count + g - g % 2 + z // 2
                pairs.append((z * group_count + g, target))
        there.append(pairs)
        back.append([(b, a) for a, b in pairs])
    return there, back


def local(
    inputs,
    clips_here,
    first_gain,
    first_shift,
    query_key_value,
    query_bias,
    value_bias,
    output_weight,
    output_bias,
    second_gain,
    second_shift,
    expand_weight,
    expand_bias,
    contract_weight,
    contract_bias,
    output_grad,
):
    slot_count, rows, width = inputs.shape
    tensor_index = lax.axis_index("tensor")
    tensor_count = lax.axis_size("tensor")
    group_index = lax.axis_index("group")
    group_count = lax.axis_size("group")
    both = ("tensor", "group")
    there, back = clip_exchange(tensor_count, group_count)
    pair = [(g, g + 1 - 2 * (g % 2)) for g in range(group_count)]

    def to_chip(array):
        pieces = []
        for turn in range(2):
            slot = (turn + tensor_index) % 2
            pieces.append(
                lax.ppermute(lax.dynamic_index_in_dim(array, slot, keepdims=False), both, there[turn])
            )
        return jnp.concatenate(pieces, axis=0)

    def to_owner(array):
        received = [
            lax.ppermute(array[turn * rows : (turn + 1) * rows], both, back[turn]) for turn in range(2)
        ]
        even = tensor_index % 2 == 0
        return jnp.stack(
            [jnp.where(even, received[0], received[1]), jnp.where(even, received[1], received[0])]
        )

    def gather(shard):
        return lax.all_gather(shard, both, axis=0).reshape(tensor_count, group_count, *shard.shape)

    alive = (jnp.arange(slot_count, dtype=jnp.int32) < clips_here[0]).astype(bf16)[:, None, None]
    tokens = to_chip(inputs).astype(f32)
    triple = gather(query_key_value).transpose(2, 1, 3, 0, 4).reshape(3, width, width)
    mixing = gather(output_weight).transpose(0, 2, 1, 3).reshape(width, width)
    up = gather(expand_weight).transpose(1, 2, 0, 3).reshape(width, -1)
    down = gather(contract_weight).transpose(0, 2, 1, 3).reshape(-1, width)
    bias_sizes = (query_bias.shape[0], value_bias.shape[0], expand_bias.shape[0])
    biases = lax.all_gather(jnp.concatenate([query_bias, value_bias, expand_bias]), "tensor", axis=0)
    query_offset = biases[:, : bias_sizes[0]].reshape(-1).astype(f32)
    value_offset = biases[:, bias_sizes[0] : bias_sizes[0] + bias_sizes[1]].reshape(-1).astype(f32)
    hidden_offset = biases[:, bias_sizes[0] + bias_sizes[1] :].reshape(-1).astype(f32)
    top = to_chip(output_grad * alive)

    gain_one = first_gain.astype(f32)
    gain_two = second_gain.astype(f32)
    first_plain, first_inverse = normalize(tokens)
    first_rows = (first_plain * gain_one + first_shift.astype(f32)).astype(bf16)
    keys = dot(first_rows, triple[1]).astype(bf16)
    values = (dot(first_rows, triple[2]) + value_offset).astype(bf16)
    far_keys = lax.ppermute(keys, "group", pair)
    far_values = lax.ppermute(values, "group", pair)
    queries = ((dot(first_rows, triple[0]) + query_offset) * query_scale).astype(bf16)
    attended, log_totals = attend_forward(queries, keys, far_keys, values, far_values)
    middle = tokens + dot(attended, mixing) + output_bias.astype(f32)
    second_plain, second_inverse = normalize(middle)
    second_rows = (second_plain * gain_two + second_shift.astype(f32)).astype(bf16)
    hidden_pre = dot(second_rows, up) + hidden_offset
    normal_cdf = 0.5 * (1.0 + lax.erf(hidden_pre * root_half))
    hidden = (hidden_pre * normal_cdf).astype(bf16)
    slope = normal_cdf + hidden_pre * (inv_root_two_pi * jnp.exp(-0.5 * hidden_pre * hidden_pre))
    output = to_owner((middle + dot(hidden, down) + contract_bias.astype(f32)).astype(bf16))

    contract_bias_part = jnp.sum(top.astype(f32), axis=0)
    contract_part = dot(hidden, top, TN)
    pre_grad = (dot(top, down, NT) * slope).astype(bf16)
    expand_bias_part = jnp.sum(pre_grad.astype(f32), axis=0)
    expand_part = dot(second_rows, pre_grad, TN)
    second_grad = dot(pre_grad, up, NT)
    second_gain_part = jnp.sum(second_grad * second_plain, axis=0)
    second_shift_part = jnp.sum(second_grad, axis=0)
    middle_grad = top.astype(f32) + normalize_back(second_grad, second_plain, second_inverse, gain_two)
    branch_grad = middle_grad.astype(bf16)
    output_bias_part = jnp.sum(branch_grad.astype(f32), axis=0)
    mixing_part = dot(attended, branch_grad, TN)
    attended_grad = dot(branch_grad, mixing, NT).astype(bf16)
    query_grad, key_own, key_far, value_own, value_far = attend_backward(
        queries, attended_grad, attended, log_totals, keys, far_keys, values, far_values
    )
    key_grad = (key_own.astype(f32) + lax.ppermute(key_far, "group", pair).astype(f32)).astype(bf16)
    value_grad = (value_own.astype(f32) + lax.ppermute(value_far, "group", pair).astype(f32)).astype(bf16)
    query_bias_part = jnp.sum(query_grad.astype(f32), axis=0)
    value_bias_part = jnp.sum(value_grad.astype(f32), axis=0)
    triple_part = jnp.stack([dot(first_rows, d, TN) for d in (query_grad, key_grad, value_grad)])
    first_grad = (
        dot(query_grad, triple[0], NT) + dot(key_grad, triple[1], NT) + dot(value_grad, triple[2], NT)
    )
    first_gain_part = jnp.sum(first_grad * first_plain, axis=0)
    first_shift_part = jnp.sum(first_grad, axis=0)
    input_grad = to_owner(
        (middle_grad + normalize_back(first_grad, first_plain, first_inverse, gain_one)).astype(bf16)
    )

    def scatter(stacked):
        count = tensor_count * group_count
        part = lax.psum_scatter(
            stacked.astype(bf16).reshape(count, *stacked.shape[2:]), both, scatter_dimension=0
        )
        return lax.psum(part, "cross").astype(f32)

    depth, across = width // group_count, width // tensor_count
    unit = expand_bias.shape[0]
    triple_sum = scatter(
        triple_part.reshape(3, group_count, depth, tensor_count, across).transpose(3, 1, 0, 2, 4)
    )
    mixing_sum = scatter(
        mixing_part.reshape(tensor_count, across, group_count, depth).transpose(0, 2, 1, 3)
    )
    expand_sum = scatter(
        expand_part.reshape(group_count, depth, tensor_count, unit).transpose(2, 0, 1, 3)
    )
    contract_sum = scatter(
        contract_part.reshape(tensor_count, unit, group_count, depth).transpose(0, 2, 1, 3)
    )
    small_sums = lax.psum(
        (
            first_gain_part,
            first_shift_part,
            query_bias_part,
            value_bias_part,
            output_bias_part,
            second_gain_part,
            second_shift_part,
            expand_bias_part,
            contract_bias_part,
        ),
        ("tensor", "group", "cross"),
    )

    def own_group(full_vector):
        size = full_vector.shape[0] // group_count
        return lax.dynamic_slice_in_dim(full_vector, group_index * size, size)

    def own_split(full_vector):
        size = full_vector.shape[0] // (group_count * tensor_count)
        return lax.dynamic_slice_in_dim(
            full_vector, (tensor_index * group_count + group_index) * size, size
        )

    return (
        output,
        input_grad,
        own_group(small_sums[0]),
        own_group(small_sums[1]),
        triple_sum,
        own_split(small_sums[2]),
        own_split(small_sums[3]),
        mixing_sum,
        own_group(small_sums[4]),
        own_group(small_sums[5]),
        own_group(small_sums[6]),
        expand_sum,
        own_split(small_sums[7]),
        contract_sum,
        own_group(small_sums[8]),
    )


def solution(mesh):
    in_specs = (
        P(("group", "cross"), "tensor", None),
        P(("group", "cross")),
        P(),
        P(),
        P(None, "group", "tensor"),
        P("tensor"),
        P("tensor"),
        P("tensor", "group"),
        P(),
        P(),
        P(),
        P("group", "tensor"),
        P("tensor"),
        P("tensor", "group"),
        P(),
        P(("group", "cross"), "tensor", None),
    )
    out_specs = (
        P(("group", "cross"), "tensor", None),
        P(("group", "cross"), "tensor", None),
        P("group"),
        P("group"),
        P(None, "group", "tensor"),
        P(("tensor", "group")),
        P(("tensor", "group")),
        P("tensor", "group"),
        P("group"),
        P("group"),
        P("group"),
        P("group", "tensor"),
        P(("tensor", "group")),
        P("tensor", "group"),
        P("group"),
    )
    return jax.shard_map(local, mesh=mesh, in_specs=in_specs, out_specs=out_specs, check_vma=False)
```

```python
import functools

import jax
import jax.numpy as jnp
from jax import lax
from jax.experimental import pallas as pl
from jax.experimental.pallas import tpu as pltpu
from jax.sharding import PartitionSpec as P

HEAD = 64
LANES = 128

epsilon = 1e-06
root_half = 0.7071067811865476
inv_root_two_pi = 0.3989422804014327
log_two = 0.6931471805599453
query_scale = HEAD**-0.5 / log_two

f32 = jnp.float32
bf16 = jnp.bfloat16

NN = (((1,), (0,)), ((), ()))
NT = (((1,), (1,)), ((), ()))
TN = (((0,), (0,)), ((), ()))


def dot(a, b, dims=NN):
    return lax.dot_general(a, b, dims, preferred_element_type=f32)


def low_lanes(array):
    return lax.broadcasted_iota(jnp.int32, array.shape, 1) < HEAD


def forward_load(rows, k, v, keys, values_low, values_high):
    low, one = low_lanes(v), jnp.ones_like(v)
    keys[rows] = k
    values_low[rows] = jnp.where(low, v, one)
    values_high[rows] = jnp.where(low, one, v)


def forward_heads(q, keys, values_low, values_high):
    low, zero = low_lanes(q), jnp.zeros_like(q)
    sums, tops = [], []
    for mine, v in ((jnp.where(low, q, zero), values_low), (jnp.where(low, zero, q), values_high)):
        s = dot(mine, keys[...], NT)
        top = jnp.max(s, axis=1, keepdims=True)
        p = jnp.exp2(s - top).astype(bf16)
        sums.append(dot(p, v[...]))
        tops.append(top)
    total = pltpu.roll(jnp.where(low, sums[1], sums[0]), HEAD, 1)
    out = (jnp.where(low, sums[0], sums[1]) / total).astype(bf16)
    return out, jnp.where(low, tops[0], tops[1]) + jnp.log2(total)


def backward_heads(q, g, o, lse, keys, values, dk, dv):
    low = low_lanes(q)
    product = g.astype(f32) * o.astype(f32)
    q_t, g_t = q.T, g.T
    dqs = []
    for h in range(2):

        def own(a):
            zero = jnp.zeros_like(a)
            return jnp.where(low, a, zero) if h == 0 else jnp.where(low, zero, a)

        inner = jnp.sum(own(product), axis=1, keepdims=True)
        p = jnp.exp2(dot(own(q), keys[...], NT) - lse[:, HEAD * h : HEAD * h + 1])
        ds = (p * (dot(own(g), values[...], NT) - inner)).astype(bf16)
        dqs.append(dot(ds, keys[...]))
        rows = slice(HEAD * h, HEAD * (h + 1))
        dv[rows] = dot(g_t[rows], p.astype(bf16))
        dk[rows] = dot(q_t[rows], ds)
    return (jnp.where(low, dqs[0], dqs[1]) * HEAD**-0.5).astype(bf16)


def key_value_total(dk, dv):
    return (dk[...] * log_two).T, dv[...].T


def attend_forward_kernel(q_ref, ka, kb, va, vb, o_ref, lse_ref, *held):
    n = ka.shape[0]
    forward_load(slice(0, n), ka[...], va[...], *held)
    forward_load(slice(n, 2 * n), kb[...], vb[...], *held)
    o_ref[...], lse_ref[...] = forward_heads(q_ref[...], *held)


def attend_backward_kernel(
    q_ref, g_ref, o_ref, lse_ref, ka, kb, va, vb,
    dq_ref, dka, dkb, dva, dvb,
    keys, values, dk, dv,
):
    n = ka.shape[0]
    for i, (k, v) in enumerate(((ka, va), (kb, vb))):
        keys[i * n : (i + 1) * n] = k[...]
        values[i * n : (i + 1) * n] = v[...]
    dq_ref[...] = backward_heads(
        q_ref[...], g_ref[...], o_ref[...], lse_ref[...], keys, values, dk, dv
    )
    key_total, value_total = key_value_total(dk, dv)
    dka[...] = key_total[:n].astype(bf16)
    dkb[...] = key_total[n:].astype(bf16)
    dva[...] = value_total[:n].astype(bf16)
    dvb[...] = value_total[n:].astype(bf16)


def attend_forward(q, ka, kb, va, vb):
    n, width = q.shape
    spec = pl.BlockSpec((n, LANES), lambda i: (0, i))
    return pl.pallas_call(
        attend_forward_kernel,
        grid=(width // LANES,),
        in_specs=[spec] * 5,
        out_specs=[spec] * 2,
        out_shape=[jax.ShapeDtypeStruct((n, width), bf16), jax.ShapeDtypeStruct((n, width), f32)],
        scratch_shapes=[pltpu.VMEM((2 * n, LANES), bf16)] * 3,
        name="attend_forward",
        cost_estimate=pl.CostEstimate(
            flops=8 * n * n * width, bytes_accessed=16 * n * width, transcendentals=n * n * width // 32
        ),
        compiler_params=pltpu.CompilerParams(vmem_limit_bytes=56 << 20),
    )(q, ka, kb, va, vb)


def attend_backward(q, g, o, lse, ka, kb, va, vb):
    n, width = q.shape
    spec = pl.BlockSpec((n, LANES), lambda i: (0, i))
    return pl.pallas_call(
        attend_backward_kernel,
        grid=(width // LANES,),
        in_specs=[spec] * 8,
        out_specs=[spec] * 5,
        out_shape=[jax.ShapeDtypeStruct((n, width), bf16)] * 5,
        scratch_shapes=[pltpu.VMEM((2 * n, LANES), bf16)] * 2 + [pltpu.VMEM((LANES, 2 * n), f32)] * 2,
        name="attend_backward",
        cost_estimate=pl.CostEstimate(
            flops=20 * n * n * width, bytes_accessed=28 * n * width, transcendentals=n * n * width // 32
        ),
        compiler_params=pltpu.CompilerParams(vmem_limit_bytes=60 << 20),
    )(q, g, o, lse, ka, kb, va, vb)


MESH = pl.DeviceIdType.MESH
AXES = ("tensor", "group", "cross")
TRIPLE, MIXING, UP, DOWN = range(4)
CORE, X, Y, NEAR, FAR = range(5)
OWN, LAST = 5, 6
HALF, PART_A, PART_B = range(3)


def place():
    t, g, x = (lax.axis_index(axis) for axis in AXES)
    return t, g // 2, g % 2, x


def depth_of(which):
    t = lax.axis_index(AXES[0])
    near = t + 1 - 2 * (t % 2)
    return {OWN: t, NEAR: near, FAR: lax.rem(t + 2, 4), LAST: lax.rem(near + 2, 4)}[which]


def peer(kind):
    t, y, c, x = place()
    if kind in (NEAR, FAR):
        t = depth_of(kind)
    elif kind == X:
        x = 1 - x
    elif kind == Y:
        y = 1 - y
    else:
        c = 1 - c
    return (t, y * 2 + c, x)


def greet(devices):
    barrier = pltpu.get_barrier_semaphore()
    for device in devices:
        pl.semaphore_signal(barrier, inc=1, device_id=device, device_id_type=MESH)
    pl.semaphore_wait(barrier, len(devices))


def remote(source, target, send, recv, device):
    return pltpu.make_async_remote_copy(
        source, target, send, recv, device_id=device, device_id_type=MESH
    )


def chip_line():
    t, y, c, x = place()
    devices = [(t, y * 2 + 1 - c, x)]
    for step in range(1, 4):
        for core in range(2):
            devices.append((lax.rem(t + step, 4), y * 2 + core, x))
    return devices


def neighbours():
    return chip_line() + [peer(X), peer(Y)]


def staged(count, stages):
    slots = []
    for now in range(count + max(delay for delay, _ in stages)):
        slots.append(
            [(stage, now - delay) for delay, stage in stages if 0 <= now - delay < count]
        )
    return slots


def run(slot):
    for stage, item in slot:
        stage(item)


class Copies:
    def go(self, m, *steps):
        for step in steps:
            self.copy(m, step).start()

    def got(self, m, *steps):
        for step in steps:
            self.copy(m, step).wait_recv()


class Weight:
    sections = {HALF: (0, 128), PART_A: (0, 48), PART_B: (48, 80)}

    def __init__(self, kind, shard, whole):
        self.kind, self.shard, self.whole = kind, shard, whole
        self.unit = 4 if kind == DOWN else 1

    def rows(self, part, half, base=0):
        off, size = self.sections[part]
        return pl.ds(pl.multiple_of(base + (half * 128 + off) * self.unit, 16), size * self.unit)

    def own(self, part, half):
        r = self.rows(part, half)
        return self.shard.at[:, r, :] if self.kind == TRIPLE else self.shard.at[r, :]

    def at(self, y, c, part, half, depth=None):
        g = y * 2 + c
        if self.kind in (TRIPLE, UP):
            n = self.shard.shape[-1]
            r = self.rows(part, half, g * 256)
            cols = slice(None) if depth is None else pl.ds(pl.multiple_of(depth * n, n), n)
            return self.whole.at[:, r, cols] if self.kind == TRIPLE else self.whole.at[r, cols]
        cols = pl.ds(pl.multiple_of(g * 256, 256), 256)
        return self.whole.at[slice(None) if depth is None else depth, self.rows(part, half), cols]


Z_NEAR, Z_FAR, Z_ON = 0, 1, 2
X_HALF = {NEAR: 3, FAR: 4, LAST: 5}
Y_HALF = {OWN: 6, NEAR: 7, FAR: 8, LAST: 9}
Y_REST = {OWN: 10, NEAR: 11, FAR: 12, LAST: 13}
X_REST = {OWN: 14, NEAR: 15, FAR: 16, LAST: 17}
TO_CORE = (18, 19, 20, 21, 22)
GATHER_STEPS = 23


class Gather(Copies):
    def __init__(self, weights, send, recv, here):
        self.weights, self.send, self.recv, self.here = weights, send, recv, here

    def copy(self, m, step):
        w = self.weights[m]
        t, y, c, x = place()
        if step in (Z_NEAR, Z_FAR):
            target = NEAR if step == Z_NEAR else FAR
            source, into = w.own(HALF, x), w.at(y, c, HALF, x, t)
        elif step == Z_ON:
            target = NEAR
            source = into = w.at(y, c, HALF, x, depth_of(FAR))
        elif step in TO_CORE:
            target = CORE
            at_y, part, half = (
                (y, HALF, x),
                (y, HALF, 1 - x),
                (1 - y, HALF, x),
                (1 - y, PART_A, 1 - x),
                (1 - y, PART_B, 1 - x),
            )[step - TO_CORE[0]]
            source = into = w.at(at_y, c, part, half)
        else:
            for steps, target, at_y, part, half in (
                (X_HALF, X, y, HALF, x),
                (Y_HALF, Y, y, HALF, x),
                (Y_REST, Y, y, PART_A, 1 - x),
                (X_REST, X, 1 - y, PART_B, x),
            ):
                depths = [which for which, k in steps.items() if k == step]
                if depths:
                    break
            source = into = w.at(at_y, c, part, half, depth_of(depths[0]))
            if step in (Y_HALF[OWN], Y_REST[OWN]):
                source = w.own(part, half)
        return remote(source, into, self.send.at[m, step], self.recv.at[m, step], peer(target))

    def own_copy(self, m, half):
        t, y, c, _ = place()
        w = self.weights[m]
        return pltpu.make_async_copy(w.own(HALF, half), w.at(y, c, HALF, half, t), self.here.at[m, half])

    def begin(self, m):
        for half in range(2):
            self.own_copy(m, half).start()
        self.go(m, Z_FAR, Z_NEAR, Y_HALF[OWN], Y_REST[OWN])

    def spread(self, m):
        self.got(m, Z_FAR)
        self.go(m, Z_ON, X_HALF[FAR], Y_HALF[FAR])
        self.got(m, Z_NEAR)
        self.go(m, X_HALF[NEAR], Y_HALF[NEAR])
        self.got(m, Y_HALF[OWN])
        self.go(m, X_REST[OWN])

    def cross(self, m):
        self.got(m, Z_ON)
        self.go(m, X_HALF[LAST], Y_HALF[LAST])
        for half in range(2):
            self.own_copy(m, half).wait()
        self.go(m, TO_CORE[0])
        for q in (FAR, NEAR):
            self.got(m, X_HALF[q])
            self.go(m, Y_REST[q])
            self.got(m, Y_HALF[q])
            self.go(m, X_REST[q])

    def finish(self, m):
        self.got(m, X_HALF[LAST])
        self.go(m, Y_REST[LAST], TO_CORE[1])
        self.got(m, Y_HALF[LAST])
        self.go(m, X_REST[LAST], TO_CORE[2])

    def share(self, m):
        self.got(m, *Y_REST.values())
        self.go(m, TO_CORE[3])
        self.got(m, *X_REST.values())
        self.go(m, TO_CORE[4])

    def end(self, m):
        self.got(m, *TO_CORE)
        for step in range(GATHER_STEPS):
            self.copy(m, step).wait_send()

    def slots(self):
        n = len(self.weights)
        return staged(
            n, ((0, self.spread), (1, self.cross), (2, self.finish), (3, self.share), (4, self.end))
        )

    @staticmethod
    def semaphores(n):
        return [
            pltpu.SemaphoreType.DMA((n, GATHER_STEPS)),
            pltpu.SemaphoreType.DMA((n, GATHER_STEPS)),
            pltpu.SemaphoreType.DMA((n, 2)),
        ]


def whole_shape(kind):
    return {TRIPLE: (3, 1024, 1024), MIXING: (4, 256, 1024), UP: (1024, 4096), DOWN: (4, 1024, 1024)}[kind]


class Turns:
    def start(self):
        for turn in range(2):
            stays, near, far = self.parts(turn)
            pl.when(stays)(near.start)
            pl.when(jnp.logical_not(stays))(far.start)

    def wait(self):
        for turn in range(2):
            stays, near, far = self.parts(turn)
            pl.when(stays)(near.wait)
            pl.when(jnp.logical_not(stays))(far.wait)

    def __init__(self, array, into, send, recv, here):
        self.array, self.into, self.send, self.recv, self.here = array, into, send, recv, here

    @staticmethod
    def semaphores():
        return [pltpu.SemaphoreType.DMA((2,))] * 3


class ToChip(Turns):
    def parts(self, turn):
        t, y, c, x = place()
        slot = lax.rem(turn + t, 2)
        source, into = self.array.at[slot], self.into.at[turn]
        target = (2 * slot + c, y * 2 + t // 2, x)
        stays = jnp.logical_and(2 * slot + c == t, t // 2 == c)
        far = remote(source, into, self.send.at[turn], self.recv.at[turn], target)
        return stays, pltpu.make_async_copy(source, into, self.here.at[turn]), far


class ToOwner(Turns):
    def parts(self, turn):
        t, y, c, x = place()
        owner = 2 * c + lax.rem(t // 2 + turn, 2)
        source, into = self.array.at[turn], self.into.at[lax.rem(turn + owner, 2)]
        stays = jnp.logical_and(owner == t, lax.rem(t, 2) == c)
        far = remote(
            source, into, self.send.at[turn], self.recv.at[turn], (owner, y * 2 + lax.rem(t, 2), x)
        )
        return stays, pltpu.make_async_copy(source, into, self.here.at[turn]), far


ANYWHERE = pl.BlockSpec(memory_space=pl.ANY)
VMEM = pl.BlockSpec(memory_space=pltpu.VMEM)


def gather_kernel(shard, inputs, bias, whole, tokens, biases, *rest):
    t, y, c, x = place()
    gather = Gather([Weight(TRIPLE, shard, whole)], *rest[:3])
    move = ToChip(inputs, tokens, *rest[3:6])
    bias_send, bias_recv, bias_here = rest[6:]
    own_bias = pltpu.make_async_copy(bias, biases.at[t], bias_here.at[0])
    bias_copies = [
        remote(bias, biases.at[t], bias_send.at[k], bias_recv.at[k], (depth_of(q), y * 2 + c, x))
        for k, q in enumerate((NEAR, FAR, LAST))
    ]
    greet(neighbours())
    own_bias.start()
    for copy in bias_copies:
        copy.start()
    gather.begin(0)
    move.start()
    for slot in gather.slots():
        run(slot)
    move.wait()
    own_bias.wait()
    for copy in bias_copies:
        copy.wait()


def gather_first(inputs, bias, shard):
    return pl.pallas_call(
        gather_kernel,
        name="gather_first",
        in_specs=[ANYWHERE] * 3,
        out_specs=[ANYWHERE] * 3,
        out_shape=[
            jax.ShapeDtypeStruct(whole_shape(TRIPLE), bf16),
            jax.ShapeDtypeStruct(inputs.shape, bf16),
            jax.ShapeDtypeStruct((4,) + bias.shape, f32),
        ],
        scratch_shapes=Gather.semaphores(1)
        + Turns.semaphores()
        + [pltpu.SemaphoreType.DMA((3,)), pltpu.SemaphoreType.DMA((3,)), pltpu.SemaphoreType.DMA((1,))],
        compiler_params=pltpu.CompilerParams(collective_id=0, has_side_effects=True),
    )(shard, inputs, bias)


X_FIRST, Y_FIRST0, Y_FIRST1, Y_SECOND, X_SECOND, Z_LAST, Z_BACK, Z_BESIDE, DONE, CORES = range(10)
SUM_STEPS = CORES + 2


def shard_shape(kind, rows, lead=()):
    return lead + {TRIPLE: (3, rows, 256), MIXING: (rows, 256), UP: (rows, 1024), DOWN: (4 * rows, 256)}[kind]


def wide_shape(kind, rows, lead=()):
    return lead + {
        TRIPLE: (3, rows, 1024),
        MIXING: (4, rows, 256),
        UP: (rows, 4096),
        DOWN: (4, 4 * rows, 256),
    }[kind]


def sum_buffers(kind):
    shapes = (
        wide_shape(kind, 256, (2,)),
        wide_shape(kind, 256, (2,)),
        wide_shape(kind, 48, (2,)),
        wide_shape(kind, 80, (2,)),
        wide_shape(kind, 48),
        wide_shape(kind, 80),
        shard_shape(kind, 128, (3,)),
        shard_shape(kind, 128),
        shard_shape(kind, 128),
    )
    return [pltpu.VMEM(s, bf16) for s in shapes]


BUFFERS = 9


class Total(Weight):
    sections = {HALF: (0, 128), PART_A: (0, 80), PART_B: (80, 48)}

    def __init__(self, kind, part, out, buffers):
        super().__init__(kind, out, part)
        self.acc, self.got_core, self.x1, self.y1, self.y2, self.x2, self.z, self.mine, self.other = buffers

    def sums(self, y, part, half, depth=None):
        r = self.rows(part, half)
        n = self.shard.shape[-1]
        cols = slice(None) if depth is None else pl.ds(pl.multiple_of(depth * n, n), n)
        if self.kind == TRIPLE:
            return self.acc.at[y, :, r, cols]
        if self.kind == UP:
            return self.acc.at[y, r, cols]
        return self.acc.at[y, slice(None) if depth is None else depth, r, :]

    def source(self, y, c):
        g = pl.ds(pl.multiple_of((y * 2 + c) * 256, 256), 256)
        if self.kind == UP:
            return self.whole.at[g, :]
        return self.whole.at[:, g, :] if self.kind == TRIPLE else self.whole.at[:, :, g]


def each(ref, body):
    lead = ref.shape[:-2]
    count = 1
    for n in lead:
        count *= n
    for i in range(count):
        index, rest = [], i
        for n in reversed(lead):
            index.insert(0, rest % n)
            rest //= n

        def step(r, carry, index=tuple(index)):
            body(index + (pl.ds(pl.multiple_of(r * 16, 16), 16),))
            return carry

        lax.fori_loop(0, ref.shape[-2] // 16, step, 0)


def add_into(into, more):
    def body(index):
        into[index] = into[index] + more[index]

    each(more, body)


class Scatter(Copies):
    def __init__(self, totals, send, recv, here):
        self.totals, self.send, self.recv, self.here = totals, send, recv, here

    def copy(self, m, step):
        w = self.totals[m]
        _, y, c, x = place()
        if step >= CORES:
            k = step - CORES
            source, into, target = w.source(k, 1 - c), w.got_core.at[k], CORE
        else:
            source, into, target = {
                X_FIRST: lambda: (w.sums(slice(None), PART_B, 1 - x), w.x1, X),
                Y_FIRST0: lambda: (w.sums(1 - y, PART_A, 0), w.y1.at[0], Y),
                Y_FIRST1: lambda: (w.sums(1 - y, PART_A, 1), w.y1.at[1], Y),
                Y_SECOND: lambda: (w.sums(1 - y, PART_B, x), w.y2, Y),
                X_SECOND: lambda: (w.sums(y, PART_A, 1 - x), w.x2, X),
                Z_LAST: lambda: (w.sums(y, HALF, x, depth_of(LAST)), w.z.at[0], NEAR),
                Z_BACK: lambda: (w.sums(y, HALF, x, depth_of(FAR)), w.z.at[1], FAR),
                Z_BESIDE: lambda: (w.sums(y, HALF, x, depth_of(NEAR)), w.z.at[2], NEAR),
                DONE: lambda: (w.mine, w.other, X),
            }[step]()
        return remote(source, into, self.send.at[m, step], self.recv.at[m, step], peer(target))

    def load(self, m, y):
        w = self.totals[m]
        return pltpu.make_async_copy(w.source(y, place()[2]), w.acc.at[y], self.here.at[m, y])

    def begin(self, m):
        for y in range(2):
            self.load(m, y).start()
            self.go(m, CORES + y)

    def cores(self, m):
        for y in range(2):
            self.load(m, y).wait()
            self.got(m, CORES + y)
        add_into(self.totals[m].acc, self.totals[m].got_core)
        self.go(m, X_FIRST, Y_FIRST0, Y_FIRST1)

    def second(self, m):
        w = self.totals[m]
        _, y, _, x = place()
        self.got(m, X_FIRST)
        add_into(w.sums(slice(None), PART_B, x), w.x1)
        self.go(m, Y_SECOND)
        self.got(m, Y_FIRST0, Y_FIRST1)
        add_into(w.sums(y, PART_A, 0), w.y1.at[0])
        add_into(w.sums(y, PART_A, 1), w.y1.at[1])
        self.go(m, X_SECOND)

    def line(self, m):
        w = self.totals[m]
        _, y, _, x = place()
        self.got(m, Y_SECOND)
        add_into(w.sums(y, PART_B, x), w.y2)
        self.got(m, X_SECOND)
        add_into(w.sums(y, PART_A, x), w.x2)
        self.go(m, Z_LAST, Z_BESIDE)

    def line_on(self, m):
        w = self.totals[m]
        _, y, _, x = place()
        self.got(m, Z_LAST)
        add_into(w.sums(y, HALF, x, depth_of(FAR)), w.z.at[0])
        self.go(m, Z_BACK)

    def own_half(self, m):
        w = self.totals[m]
        _, y, _, x = place()
        self.got(m, Z_BESIDE, Z_BACK)
        own, near, far = w.sums(y, HALF, x, depth_of(OWN)), w.z.at[2], w.z.at[1]
        out = w.own(HALF, x)

        def body(index):
            total = (own[index].astype(f32) + near[index].astype(f32) + far[index].astype(f32)).astype(bf16)
            w.mine[index] = total
            out[index] = total.astype(f32)

        each(w.mine, body)
        self.go(m, DONE)

    def other_half(self, m):
        w = self.totals[m]
        self.got(m, DONE)
        out = w.own(HALF, 1 - place()[3])

        def body(index):
            out[index] = w.other[index].astype(f32)

        each(w.other, body)
        for step in range(SUM_STEPS):
            self.copy(m, step).wait_send()

    def slots(self):
        stages = (self.cores, self.second, self.line, self.line_on, self.own_half, self.other_half)
        return staged(len(self.totals), tuple(enumerate(stages)))

    @staticmethod
    def semaphores(n):
        return [
            pltpu.SemaphoreType.DMA((n, SUM_STEPS)),
            pltpu.SemaphoreType.DMA((n, SUM_STEPS)),
            pltpu.SemaphoreType.DMA((n, 2)),
        ]


AROUND = (CORE, X, Y, NEAR, FAR)


def scatter_kernel(kinds, *refs):
    n = len(kinds)
    parts, small, tokens = refs[:n], refs[n], refs[n + 1]
    outs, small_out, slots = refs[n + 2 : 2 * n + 2], refs[2 * n + 2], refs[2 * n + 3]
    rest = refs[2 * n + 4 :]
    buffers, rest = rest[: BUFFERS * n], rest[BUFFERS * n :]
    sums, arrived, small_send, small_recv = rest[:4]
    move = ToOwner(tokens, slots, *rest[4:7])
    scatter = Scatter(
        [Total(kind, parts[i], outs[i], buffers[BUFFERS * i :][:BUFFERS]) for i, kind in enumerate(kinds)],
        *rest[7:],
    )

    def small_copy(k):
        return remote(sums.at[k], arrived.at[k], small_send.at[k], small_recv.at[k], peer(AROUND[k]))

    greet(neighbours())
    for m in range(n):
        scatter.begin(m)
    move.start()
    sums[0] = small[...]
    small_copy(0).start()
    for k, slot in enumerate(scatter.slots()):
        run(slot)
        if k < len(AROUND):
            small_copy(k).wait_recv()
            sums[k + 1] = sums[k] + arrived[k]
            if k + 1 < len(AROUND):
                small_copy(k + 1).start()
    small_out[...] = sums[len(AROUND)]
    for k in range(len(AROUND)):
        small_copy(k).wait_send()
    move.wait()


def scatter_last(kinds, parts, small, tokens):
    n = len(kinds)
    scratch = sum((sum_buffers(kind) for kind in kinds), [])
    scratch += [
        pltpu.VMEM((len(AROUND) + 1,) + small.shape, f32),
        pltpu.VMEM((len(AROUND),) + small.shape, f32),
        pltpu.SemaphoreType.DMA((len(AROUND),)),
        pltpu.SemaphoreType.DMA((len(AROUND),)),
    ]
    return pl.pallas_call(
        functools.partial(scatter_kernel, kinds),
        name="scatter_last",
        in_specs=[ANYWHERE] * n + [VMEM, ANYWHERE],
        out_specs=[VMEM] * (n + 1) + [ANYWHERE],
        out_shape=[jax.ShapeDtypeStruct(shard_shape(kind, 256), f32) for kind in kinds]
        + [jax.ShapeDtypeStruct(small.shape, f32), jax.ShapeDtypeStruct(tokens.shape, bf16)],
        scratch_shapes=scratch + Turns.semaphores() + Scatter.semaphores(n),
        compiler_params=pltpu.CompilerParams(
            collective_id=1, has_side_effects=True, vmem_limit_bytes=60 << 20
        ),
    )(*parts, small, tokens)


def at_step(step, slots_at, slots):
    for when in sorted(set(slots_at)):

        @pl.when(step == when)
        def _(when=when):
            for place_at, slot in zip(slots_at, slots):
                if place_at == when:
                    run(slot)


GATHERED = (MIXING, UP, DOWN)
GATHER_AT = (1, 3, 5, 6, 7, 7, 7)


def forward_kernel(
    q_ref, ka, va, k_own, v_own, top, s0, s1, s2,
    o_ref, lse_ref, kb, vb, clip_top, w0, w1, w2,
    keys, values_low, values_high, k_far, v_far, pair_send, pair_recv, *rest,
):
    n = ka.shape[0]
    step, last = pl.program_id(0), pl.num_programs(0) - 1
    gather = Gather([Weight(*w) for w in zip(GATHERED, (s0, s1, s2), (w0, w1, w2))], *rest[:3])
    move = ToChip(top, clip_top, *rest[3:6])

    def pair(which, i):
        cols = pl.ds(pl.multiple_of(i * LANES, LANES), LANES)
        own, far = ((k_own, k_far), (v_own, v_far))[which]
        return remote(
            own.at[:, cols], far.at[:, cols], pair_send.at[which, i], pair_recv.at[which, i], peer(CORE)
        )

    @pl.when(step == 0)
    def _():
        greet(neighbours())
        for i in range(k_far.shape[1] // LANES):
            pair(0, i).start()
            pair(1, i).start()
        for m in range(len(GATHERED)):
            gather.begin(m)
        move.start()

    held = (keys, values_low, values_high)
    forward_load(slice(0, n), ka[...], va[...], *held)
    cols = pl.ds(pl.multiple_of(step * LANES, LANES), LANES)
    pair(0, step).wait_recv()
    pair(1, step).wait_recv()
    kb[...], vb[...] = k_far[:, cols], v_far[:, cols]
    forward_load(slice(n, 2 * n), kb[...], vb[...], *held)
    o_ref[...], lse_ref[...] = forward_heads(q_ref[...], *held)

    at_step(step, GATHER_AT, gather.slots())

    @pl.when(step == last)
    def _():
        for i in range(k_far.shape[1] // LANES):
            pair(0, i).wait_send()
            pair(1, i).wait_send()
        move.wait()


def attend_and_gather(q, k, v, top, shards):
    n, width = q.shape
    spec = pl.BlockSpec((n, LANES), lambda i: (0, i))
    blocks = width // LANES
    return pl.pallas_call(
        forward_kernel,
        grid=(blocks,),
        in_specs=[spec] * 3 + [ANYWHERE] * 6,
        out_specs=[spec] * 4 + [ANYWHERE] * 4,
        out_shape=[jax.ShapeDtypeStruct((n, width), bf16), jax.ShapeDtypeStruct((n, width), f32)]
        + [jax.ShapeDtypeStruct((n, width), bf16)] * 2
        + [jax.ShapeDtypeStruct(top.shape, bf16)]
        + [jax.ShapeDtypeStruct(whole_shape(kind), bf16) for kind in GATHERED],
        scratch_shapes=[pltpu.VMEM((2 * n, LANES), bf16)] * 3
        + [pltpu.VMEM((n, width), bf16)] * 2
        + [pltpu.SemaphoreType.DMA((2, blocks))] * 2
        + Gather.semaphores(len(GATHERED))
        + Turns.semaphores(),
        name="attend_and_gather",
        cost_estimate=pl.CostEstimate(
            flops=8 * n * n * width, bytes_accessed=16 * n * width, transcendentals=n * n * width // 32
        ),
        compiler_params=pltpu.CompilerParams(
            collective_id=2, has_side_effects=True, vmem_limit_bytes=56 << 20
        ),
    )(q, k, v, k, v, top, *shards)


SCATTERED = (DOWN, UP)
SCATTER_AT = (2, 3, 6, 7, 7, 7, 7)


def backward_kernel(
    q_ref, g_ref, o_ref, lse_ref, ka, kb, va, vb, output, p0, p1,
    dq_ref, dk_ref, dv_ref, slots, out0, out1,
    keys, values, dk, dv, far, got, pair_send, pair_recv, *rest,
):
    n = ka.shape[0]
    step, last = pl.program_id(0), pl.num_programs(0) - 1
    buffers, rest = rest[: BUFFERS * 2], rest[BUFFERS * 2 :]
    move = ToOwner(output, slots, *rest[:3])
    scatter = Scatter(
        [Total(DOWN, p0, out0, buffers[:BUFFERS]), Total(UP, p1, out1, buffers[BUFFERS:])], *rest[3:]
    )

    def pair(i):
        return remote(
            far.at[lax.rem(i, 2)], got.at[i], pair_send.at[lax.rem(i, 2)], pair_recv.at[i], peer(CORE)
        )

    @pl.when(step == 0)
    def _():
        greet(neighbours())
        for m in range(len(SCATTERED)):
            scatter.begin(m)
        move.start()

    for i, (k, v) in enumerate(((ka, va), (kb, vb))):
        keys[i * n : (i + 1) * n] = k[...]
        values[i * n : (i + 1) * n] = v[...]
    dq_ref[...] = backward_heads(
        q_ref[...], g_ref[...], o_ref[...], lse_ref[...], keys, values, dk, dv
    )

    def settle(i):
        cols = pl.ds(pl.multiple_of(i * LANES, LANES), LANES)
        pair(i).wait_recv()
        dk_ref[:, cols] = (dk_ref[:, cols].astype(f32) + got[i, 0].astype(f32)).astype(bf16)
        dv_ref[:, cols] = (dv_ref[:, cols].astype(f32) + got[i, 1].astype(f32)).astype(bf16)

    key_total, value_total = key_value_total(dk, dv)
    cols = pl.ds(pl.multiple_of(step * LANES, LANES), LANES)
    slot = lax.rem(step, 2)
    dk_ref[:, cols] = key_total[:n].astype(bf16)
    dv_ref[:, cols] = value_total[:n].astype(bf16)

    @pl.when(step >= 2)
    def _():
        pair(step - 2).wait_send()

    far[slot, 0] = key_total[n:].astype(bf16)
    far[slot, 1] = value_total[n:].astype(bf16)
    pair(step).start()

    @pl.when(step >= 1)
    def _():
        settle(step - 1)

    at_step(step, SCATTER_AT, scatter.slots())

    @pl.when(step == last)
    def _():
        settle(last)
        pair(last - 1).wait_send()
        pair(last).wait_send()
        move.wait()


def attend_and_scatter(q, g, o, lse, ka, kb, va, vb, output, parts):
    n, width = q.shape
    spec = pl.BlockSpec((n, LANES), lambda i: (0, i))
    blocks = width // LANES
    return pl.pallas_call(
        backward_kernel,
        grid=(blocks,),
        in_specs=[spec] * 8 + [ANYWHERE] * 3,
        out_specs=[spec] + [VMEM] * 2 + [ANYWHERE] + [VMEM] * 2,
        out_shape=[jax.ShapeDtypeStruct((n, width), bf16)] * 3
        + [jax.ShapeDtypeStruct(output.shape, bf16)]
        + [jax.ShapeDtypeStruct(shard_shape(kind, 256), f32) for kind in SCATTERED],
        scratch_shapes=[pltpu.VMEM((2 * n, LANES), bf16)] * 2
        + [pltpu.VMEM((LANES, 2 * n), f32)] * 2
        + [pltpu.VMEM((2, 2, n, LANES), bf16), pltpu.VMEM((blocks, 2, n, LANES), bf16)]
        + [pltpu.SemaphoreType.DMA((2,)), pltpu.SemaphoreType.DMA((blocks,))]
        + sum_buffers(DOWN)
        + sum_buffers(UP)
        + Turns.semaphores()
        + Scatter.semaphores(len(SCATTERED)),
        name="attend_and_scatter",
        cost_estimate=pl.CostEstimate(
            flops=20 * n * n * width, bytes_accessed=28 * n * width, transcendentals=n * n * width // 32
        ),
        compiler_params=pltpu.CompilerParams(
            collective_id=3, has_side_effects=True, vmem_limit_bytes=62 << 20
        ),
    )(q, g, o, lse, ka, kb, va, vb, output, *parts)


def normalize(values):
    center = values - jnp.mean(values, axis=-1, keepdims=True)
    inverse = lax.rsqrt(jnp.mean(center * center, axis=-1, keepdims=True) + epsilon)
    return (center * inverse, inverse)


def normalize_back(upstream, normed, inverse, norm_gain):
    scaled = upstream * norm_gain
    return inverse * (
        scaled
        - jnp.mean(scaled, axis=-1, keepdims=True)
        - normed * jnp.mean(scaled * normed, axis=-1, keepdims=True)
    )


def clip_exchange(tensor_count, group_count):
    there, back = [], []
    for turn in range(2):
        pairs = []
        for z in range(tensor_count):
            for g in range(group_count):
                slot = (turn + z) % 2
                target = (2 * slot + g % 2) * group_count + g - g % 2 + z // 2
                pairs.append((z * group_count + g, target))
        there.append(pairs)
        back.append([(b, a) for a, b in pairs])
    return there, back


def local(
    inputs,
    clips_here,
    first_gain,
    first_shift,
    query_key_value,
    query_bias,
    value_bias,
    output_weight,
    output_bias,
    second_gain,
    second_shift,
    expand_weight,
    expand_bias,
    contract_weight,
    contract_bias,
    output_grad,
):
    slot_count, rows, width = inputs.shape
    tensor_index = lax.axis_index("tensor")
    tensor_count = lax.axis_size("tensor")
    group_index = lax.axis_index("group")
    group_count = lax.axis_size("group")
    both = ("tensor", "group")
    there, back = clip_exchange(tensor_count, group_count)
    pair = [(g, g + 1 - 2 * (g % 2)) for g in range(group_count)]

    def to_chip(array):
        pieces = []
        for turn in range(2):
            slot = (turn + tensor_index) % 2
            pieces.append(
                lax.ppermute(lax.dynamic_index_in_dim(array, slot, keepdims=False), both, there[turn])
            )
        return jnp.concatenate(pieces, axis=0)

    def to_owner(array):
        received = [
            lax.ppermute(array[turn * rows : (turn + 1) * rows], both, back[turn]) for turn in range(2)
        ]
        even = tensor_index % 2 == 0
        return jnp.stack(
            [jnp.where(even, received[0], received[1]), jnp.where(even, received[1], received[0])]
        )

    def gather(shard):
        return lax.all_gather(shard, both, axis=0).reshape(tensor_count, group_count, *shard.shape)

    direct = (tensor_count, group_count, lax.axis_size("cross")) == (4, 4, 2)
    alive = (jnp.arange(slot_count, dtype=jnp.int32) < clips_here[0]).astype(bf16)[:, None, None]
    bias = jnp.concatenate([query_bias, value_bias, expand_bias])
    if direct:
        bias_size = bias.shape[0]
        bias = jnp.pad(bias.astype(f32), (0, -bias_size % (8 * LANES))).reshape(-1, LANES)
        triple, tokens, biases = gather_first(inputs, bias, query_key_value)
        tokens = tokens.reshape(-1, width).astype(f32)
        biases = biases.reshape(tensor_count, -1)[:, :bias_size]
    else:
        tokens = to_chip(inputs).astype(f32)
        triple = gather(query_key_value).transpose(2, 1, 3, 0, 4).reshape(3, width, width)
        mixing = gather(output_weight).transpose(0, 2, 1, 3).reshape(width, width)
        up = gather(expand_weight).transpose(1, 2, 0, 3).reshape(width, -1)
        down = gather(contract_weight).transpose(0, 2, 1, 3).reshape(-1, width)
        biases = lax.all_gather(bias, "tensor", axis=0).astype(f32)
    split_at = (query_bias.shape[0], query_bias.shape[0] + value_bias.shape[0])
    query_offset, value_offset, hidden_offset = (
        part.reshape(-1) for part in jnp.split(biases, split_at, axis=1)
    )

    gain_one = first_gain.astype(f32)
    gain_two = second_gain.astype(f32)
    first_plain, first_inverse = normalize(tokens)
    first_rows = (first_plain * gain_one + first_shift.astype(f32)).astype(bf16)
    keys = dot(first_rows, triple[1]).astype(bf16)
    values = (dot(first_rows, triple[2]) + value_offset).astype(bf16)
    queries = ((dot(first_rows, triple[0]) + query_offset) * query_scale).astype(bf16)
    if direct:
        attended, log_totals, far_keys, far_values, top, mixing, up, down = attend_and_gather(
            queries, keys, values, output_grad * alive, (output_weight, expand_weight, contract_weight)
        )
        top, mixing, down = top.reshape(-1, width), mixing.reshape(-1, width), down.reshape(-1, width)
    else:
        top = to_chip(output_grad * alive)
        far_keys = lax.ppermute(keys, "group", pair)
        far_values = lax.ppermute(values, "group", pair)
        attended, log_totals = attend_forward(queries, keys, far_keys, values, far_values)
    middle = tokens + dot(attended, mixing) + output_bias.astype(f32)
    second_plain, second_inverse = normalize(middle)
    second_rows = (second_plain * gain_two + second_shift.astype(f32)).astype(bf16)
    hidden_pre = dot(second_rows, up) + hidden_offset
    normal_cdf = 0.5 * (1.0 + lax.erf(hidden_pre * root_half))
    hidden = (hidden_pre * normal_cdf).astype(bf16)
    slope = normal_cdf + hidden_pre * (inv_root_two_pi * jnp.exp(-0.5 * hidden_pre * hidden_pre))
    output = (middle + dot(hidden, down) + contract_bias.astype(f32)).astype(bf16)

    contract_bias_part = jnp.sum(top.astype(f32), axis=0)
    contract_part = dot(hidden, top, TN).astype(bf16)
    pre_grad = (dot(top, down, NT) * slope).astype(bf16)
    expand_bias_part = jnp.sum(pre_grad.astype(f32), axis=0)
    expand_part = dot(second_rows, pre_grad, TN).astype(bf16)
    second_grad = dot(pre_grad, up, NT)
    second_gain_part = jnp.sum(second_grad * second_plain, axis=0)
    second_shift_part = jnp.sum(second_grad, axis=0)
    middle_grad = top.astype(f32) + normalize_back(second_grad, second_plain, second_inverse, gain_two)
    branch_grad = middle_grad.astype(bf16)
    output_bias_part = jnp.sum(branch_grad.astype(f32), axis=0)
    mixing_part = dot(attended, branch_grad, TN).astype(bf16)
    attended_grad = dot(branch_grad, mixing, NT).astype(bf16)
    if direct:
        query_grad, key_grad, value_grad, output, contract_sum, expand_sum = attend_and_scatter(
            queries, attended_grad, attended, log_totals, keys, far_keys, values, far_values,
            output.reshape(inputs.shape), (contract_part.reshape(4, -1, width), expand_part),
        )
    else:
        output = to_owner(output)
        query_grad, key_own, key_far, value_own, value_far = attend_backward(
            queries, attended_grad, attended, log_totals, keys, far_keys, values, far_values
        )
        key_grad = (key_own.astype(f32) + lax.ppermute(key_far, "group", pair).astype(f32)).astype(bf16)
        value_grad = (value_own.astype(f32) + lax.ppermute(value_far, "group", pair).astype(f32)).astype(
            bf16
        )
    query_bias_part = jnp.sum(query_grad.astype(f32), axis=0)
    value_bias_part = jnp.sum(value_grad.astype(f32), axis=0)
    triple_part = jnp.stack(
        [dot(first_rows, d, TN).astype(bf16) for d in (query_grad, key_grad, value_grad)]
    )
    first_grad = (
        dot(query_grad, triple[0], NT) + dot(key_grad, triple[1], NT) + dot(value_grad, triple[2], NT)
    )
    first_gain_part = jnp.sum(first_grad * first_plain, axis=0)
    first_shift_part = jnp.sum(first_grad, axis=0)
    input_grad = (
        middle_grad + normalize_back(first_grad, first_plain, first_inverse, gain_one)
    ).astype(bf16)

    small_parts = (
        first_gain_part,
        first_shift_part,
        query_bias_part,
        value_bias_part,
        output_bias_part,
        second_gain_part,
        second_shift_part,
        expand_bias_part,
        contract_bias_part,
    )
    if direct:
        mixing_sum, triple_sum, small, input_grad = scatter_last(
            (MIXING, TRIPLE),
            (mixing_part.reshape(4, -1, width), triple_part),
            jnp.concatenate(small_parts).reshape(-1, LANES),
            input_grad.reshape(inputs.shape),
        )
        small, small_sums = small.reshape(-1), []
        for part in small_parts:
            small_sums.append(small[: part.shape[0]])
            small = small[part.shape[0] :]
    else:
        input_grad = to_owner(input_grad)

        def scatter(stacked):
            count = tensor_count * group_count
            part = lax.psum_scatter(stacked.reshape(count, *stacked.shape[2:]), both, scatter_dimension=0)
            return lax.psum(part, "cross").astype(f32)

        depth, across = width // group_count, width // tensor_count
        unit = expand_bias.shape[0]
        triple_sum = scatter(
            triple_part.reshape(3, group_count, depth, tensor_count, across).transpose(3, 1, 0, 2, 4)
        )
        mixing_sum = scatter(
            mixing_part.reshape(tensor_count, across, group_count, depth).transpose(0, 2, 1, 3)
        )
        expand_sum = scatter(
            expand_part.reshape(group_count, depth, tensor_count, unit).transpose(2, 0, 1, 3)
        )
        contract_sum = scatter(
            contract_part.reshape(tensor_count, unit, group_count, depth).transpose(0, 2, 1, 3)
        )
        small_sums = lax.psum(small_parts, ("tensor", "group", "cross"))

    def own_group(full_vector):
        size = full_vector.shape[0] // group_count
        return lax.dynamic_slice_in_dim(full_vector, group_index * size, size)

    def own_split(full_vector):
        size = full_vector.shape[0] // (group_count * tensor_count)
        return lax.dynamic_slice_in_dim(
            full_vector, (tensor_index * group_count + group_index) * size, size
        )

    return (
        output,
        input_grad,
        own_group(small_sums[0]),
        own_group(small_sums[1]),
        triple_sum,
        own_split(small_sums[2]),
        own_split(small_sums[3]),
        mixing_sum,
        own_group(small_sums[4]),
        own_group(small_sums[5]),
        own_group(small_sums[6]),
        expand_sum,
        own_split(small_sums[7]),
        contract_sum,
        own_group(small_sums[8]),
    )


def solution(mesh):
    in_specs = (
        P(("group", "cross"), "tensor", None),
        P(("group", "cross")),
        P(),
        P(),
        P(None, "group", "tensor"),
        P("tensor"),
        P("tensor"),
        P("tensor", "group"),
        P(),
        P(),
        P(),
        P("group", "tensor"),
        P("tensor"),
        P("tensor", "group"),
        P(),
        P(("group", "cross"), "tensor", None),
    )
    out_specs = (
        P(("group", "cross"), "tensor", None),
        P(("group", "cross"), "tensor", None),
        P("group"),
        P("group"),
        P(None, "group", "tensor"),
        P(("tensor", "group")),
        P(("tensor", "group")),
        P("tensor", "group"),
        P("group"),
        P("group"),
        P("group"),
        P("group", "tensor"),
        P(("tensor", "group")),
        P("tensor", "group"),
        P("group"),
    )
    return jax.shard_map(local, mesh=mesh, in_specs=in_specs, out_specs=out_specs, check_vma=False)
```

```python
import functools

import jax
import jax.numpy as jnp
from jax import lax
from jax.experimental import pallas as pl
from jax.experimental.pallas import tpu as pltpu
from jax.sharding import PartitionSpec as P

HEAD = 64
LANES = 128

epsilon = 1e-06
root_half = 0.7071067811865476
inv_root_two_pi = 0.3989422804014327
log_two = 0.6931471805599453
query_scale = HEAD**-0.5 / log_two

f32 = jnp.float32
bf16 = jnp.bfloat16

NN = (((1,), (0,)), ((), ()))
NT = (((1,), (1,)), ((), ()))
TN = (((0,), (0,)), ((), ()))


def dot(a, b, dims=NN):
    return lax.dot_general(a, b, dims, preferred_element_type=f32)


def low_lanes(array):
    return lax.broadcasted_iota(jnp.int32, array.shape, 1) < HEAD


def forward_load(rows, k, v, keys, values_low, values_high):
    low, one = low_lanes(v), jnp.ones_like(v)
    keys[rows] = k
    values_low[rows] = jnp.where(low, v, one)
    values_high[rows] = jnp.where(low, one, v)


def forward_heads(q, keys, values_low, values_high):
    low, zero = low_lanes(q), jnp.zeros_like(q)
    sums, tops = [], []
    for mine, v in ((jnp.where(low, q, zero), values_low), (jnp.where(low, zero, q), values_high)):
        s = dot(mine, keys[...], NT)
        top = jnp.max(s, axis=1, keepdims=True)
        p = jnp.exp2(s - top).astype(bf16)
        sums.append(dot(p, v[...]))
        tops.append(top)
    total = pltpu.roll(jnp.where(low, sums[1], sums[0]), HEAD, 1)
    out = (jnp.where(low, sums[0], sums[1]) / total).astype(bf16)
    return out, jnp.where(low, tops[0], tops[1]) + jnp.log2(total)


def backward_heads(q, g, o, lse, keys, values, dk, dv):
    low = low_lanes(q)
    product = g.astype(f32) * o.astype(f32)
    q_t, g_t = q.T, g.T
    dqs = []
    for h in range(2):

        def own(a):
            zero = jnp.zeros_like(a)
            return jnp.where(low, a, zero) if h == 0 else jnp.where(low, zero, a)

        inner = jnp.sum(own(product), axis=1, keepdims=True)
        p = jnp.exp2(dot(own(q), keys[...], NT) - lse[:, HEAD * h : HEAD * h + 1])
        ds = (p * (dot(own(g), values[...], NT) - inner)).astype(bf16)
        dqs.append(dot(ds, keys[...]))
        rows = slice(HEAD * h, HEAD * (h + 1))
        dv[rows] = dot(g_t[rows], p.astype(bf16))
        dk[rows] = dot(q_t[rows], ds)
    return (jnp.where(low, dqs[0], dqs[1]) * HEAD**-0.5).astype(bf16)


def key_value_total(dk, dv):
    return (dk[...] * log_two).T, dv[...].T


def attend_forward_kernel(q_ref, ka, kb, va, vb, o_ref, lse_ref, *held):
    n = ka.shape[0]
    forward_load(slice(0, n), ka[...], va[...], *held)
    forward_load(slice(n, 2 * n), kb[...], vb[...], *held)
    o_ref[...], lse_ref[...] = forward_heads(q_ref[...], *held)


def attend_backward_kernel(
    q_ref, g_ref, o_ref, lse_ref, ka, kb, va, vb,
    dq_ref, dka, dkb, dva, dvb,
    keys, values, dk, dv,
):
    n = ka.shape[0]
    for i, (k, v) in enumerate(((ka, va), (kb, vb))):
        keys[i * n : (i + 1) * n] = k[...]
        values[i * n : (i + 1) * n] = v[...]
    dq_ref[...] = backward_heads(
        q_ref[...], g_ref[...], o_ref[...], lse_ref[...], keys, values, dk, dv
    )
    key_total, value_total = key_value_total(dk, dv)
    dka[...] = key_total[:n].astype(bf16)
    dkb[...] = key_total[n:].astype(bf16)
    dva[...] = value_total[:n].astype(bf16)
    dvb[...] = value_total[n:].astype(bf16)


def attend_forward(q, ka, kb, va, vb):
    n, width = q.shape
    spec = pl.BlockSpec((n, LANES), lambda i: (0, i))
    return pl.pallas_call(
        attend_forward_kernel,
        grid=(width // LANES,),
        in_specs=[spec] * 5,
        out_specs=[spec] * 2,
        out_shape=[jax.ShapeDtypeStruct((n, width), bf16), jax.ShapeDtypeStruct((n, width), f32)],
        scratch_shapes=[pltpu.VMEM((2 * n, LANES), bf16)] * 3,
        name="attend_forward",
        cost_estimate=pl.CostEstimate(
            flops=8 * n * n * width, bytes_accessed=16 * n * width, transcendentals=n * n * width // 32
        ),
        compiler_params=pltpu.CompilerParams(vmem_limit_bytes=56 << 20),
    )(q, ka, kb, va, vb)


def attend_backward(q, g, o, lse, ka, kb, va, vb):
    n, width = q.shape
    spec = pl.BlockSpec((n, LANES), lambda i: (0, i))
    return pl.pallas_call(
        attend_backward_kernel,
        grid=(width // LANES,),
        in_specs=[spec] * 8,
        out_specs=[spec] * 5,
        out_shape=[jax.ShapeDtypeStruct((n, width), bf16)] * 5,
        scratch_shapes=[pltpu.VMEM((2 * n, LANES), bf16)] * 2 + [pltpu.VMEM((LANES, 2 * n), f32)] * 2,
        name="attend_backward",
        cost_estimate=pl.CostEstimate(
            flops=20 * n * n * width, bytes_accessed=28 * n * width, transcendentals=n * n * width // 32
        ),
        compiler_params=pltpu.CompilerParams(vmem_limit_bytes=60 << 20),
    )(q, g, o, lse, ka, kb, va, vb)


MESH = pl.DeviceIdType.MESH
AXES = ("tensor", "group", "cross")
TRIPLE, MIXING, UP, DOWN = range(4)
CORE, X, Y, NEAR, FAR = range(5)
OWN, LAST = 5, 6
HALF, PART_A, PART_B = range(3)


def place():
    t, g, x = (lax.axis_index(axis) for axis in AXES)
    return t, g // 2, g % 2, x


def depth_of(which):
    t = lax.axis_index(AXES[0])
    near = t + 1 - 2 * (t % 2)
    return {OWN: t, NEAR: near, FAR: lax.rem(t + 2, 4), LAST: lax.rem(near + 2, 4)}[which]


def peer(kind):
    t, y, c, x = place()
    if kind in (NEAR, FAR):
        t = depth_of(kind)
    elif kind == X:
        x = 1 - x
    elif kind == Y:
        y = 1 - y
    else:
        c = 1 - c
    return (t, y * 2 + c, x)


def greet(devices):
    barrier = pltpu.get_barrier_semaphore()
    for device in devices:
        pl.semaphore_signal(barrier, inc=1, device_id=device, device_id_type=MESH)
    pl.semaphore_wait(barrier, len(devices))


def remote(source, target, send, recv, device):
    return pltpu.make_async_remote_copy(
        source, target, send, recv, device_id=device, device_id_type=MESH
    )


def chip_line():
    t, y, c, x = place()
    devices = [(t, y * 2 + 1 - c, x)]
    for step in range(1, 4):
        for core in range(2):
            devices.append((lax.rem(t + step, 4), y * 2 + core, x))
    return devices


def neighbours():
    return chip_line() + [peer(X), peer(Y)]


def staged(count, stages):
    slots = []
    for now in range(count + max(delay for delay, _ in stages)):
        slots.append(
            [(stage, now - delay) for delay, stage in stages if 0 <= now - delay < count]
        )
    return slots


def run(slot):
    for stage, item in slot:
        stage(item)


class Copies:
    def go(self, m, *steps):
        for step in steps:
            self.copy(m, step).start()

    def got(self, m, *steps):
        for step in steps:
            self.copy(m, step).wait_recv()


class Weight:
    sections = {HALF: (0, 128), PART_A: (0, 48), PART_B: (48, 80)}

    def __init__(self, kind, shard, whole):
        self.kind, self.shard, self.whole = kind, shard, whole
        self.unit = 4 if kind == DOWN else 1

    def rows(self, part, half, base=0):
        off, size = self.sections[part]
        return pl.ds(pl.multiple_of(base + (half * 128 + off) * self.unit, 16), size * self.unit)

    def own(self, part, half):
        r = self.rows(part, half)
        return self.shard.at[:, r, :] if self.kind == TRIPLE else self.shard.at[r, :]

    def at(self, y, c, part, half, depth=None):
        g = y * 2 + c
        if self.kind in (TRIPLE, UP):
            n = self.shard.shape[-1]
            r = self.rows(part, half, g * 256)
            cols = slice(None) if depth is None else pl.ds(pl.multiple_of(depth * n, n), n)
            return self.whole.at[:, r, cols] if self.kind == TRIPLE else self.whole.at[r, cols]
        cols = pl.ds(pl.multiple_of(g * 256, 256), 256)
        return self.whole.at[slice(None) if depth is None else depth, self.rows(part, half), cols]


Z_NEAR, Z_FAR, Z_ON = 0, 1, 2
X_HALF = {NEAR: 3, FAR: 4, LAST: 5}
Y_HALF = {OWN: 6, NEAR: 7, FAR: 8, LAST: 9}
Y_REST = {OWN: 10, NEAR: 11, FAR: 12, LAST: 13}
X_REST = {OWN: 14, NEAR: 15, FAR: 16, LAST: 17}
TO_CORE = (18, 19, 20, 21, 22)
GATHER_STEPS = 23


class Gather(Copies):
    def __init__(self, weights, send, recv, here):
        self.weights, self.send, self.recv, self.here = weights, send, recv, here

    def copy(self, m, step):
        w = self.weights[m]
        t, y, c, x = place()
        if step in (Z_NEAR, Z_FAR):
            target = NEAR if step == Z_NEAR else FAR
            source, into = w.own(HALF, x), w.at(y, c, HALF, x, t)
        elif step == Z_ON:
            target = NEAR
            source = into = w.at(y, c, HALF, x, depth_of(FAR))
        elif step in TO_CORE:
            target = CORE
            at_y, part, half = (
                (y, HALF, x),
                (y, HALF, 1 - x),
                (1 - y, HALF, x),
                (1 - y, PART_A, 1 - x),
                (1 - y, PART_B, 1 - x),
            )[step - TO_CORE[0]]
            source = into = w.at(at_y, c, part, half)
        else:
            for steps, target, at_y, part, half in (
                (X_HALF, X, y, HALF, x),
                (Y_HALF, Y, y, HALF, x),
                (Y_REST, Y, y, PART_A, 1 - x),
                (X_REST, X, 1 - y, PART_B, x),
            ):
                depths = [which for which, k in steps.items() if k == step]
                if depths:
                    break
            source = into = w.at(at_y, c, part, half, depth_of(depths[0]))
            if step in (Y_HALF[OWN], Y_REST[OWN]):
                source = w.own(part, half)
        return remote(source, into, self.send.at[m, step], self.recv.at[m, step], peer(target))

    def own_copy(self, m, half):
        t, y, c, _ = place()
        w = self.weights[m]
        return pltpu.make_async_copy(w.own(HALF, half), w.at(y, c, HALF, half, t), self.here.at[m, half])

    def begin(self, m):
        for half in range(2):
            self.own_copy(m, half).start()
        self.go(m, Z_FAR, Z_NEAR, Y_HALF[OWN], Y_REST[OWN])

    def spread(self, m):
        self.got(m, Z_FAR)
        self.go(m, Z_ON, X_HALF[FAR], Y_HALF[FAR])
        self.got(m, Z_NEAR)
        self.go(m, X_HALF[NEAR], Y_HALF[NEAR])
        self.got(m, Y_HALF[OWN])
        self.go(m, X_REST[OWN])

    def cross(self, m):
        self.got(m, Z_ON)
        self.go(m, X_HALF[LAST], Y_HALF[LAST])
        for half in range(2):
            self.own_copy(m, half).wait()
        self.go(m, TO_CORE[0])
        for q in (FAR, NEAR):
            self.got(m, X_HALF[q])
            self.go(m, Y_REST[q])
            self.got(m, Y_HALF[q])
            self.go(m, X_REST[q])

    def finish(self, m):
        self.got(m, X_HALF[LAST])
        self.go(m, Y_REST[LAST], TO_CORE[1])
        self.got(m, Y_HALF[LAST])
        self.go(m, X_REST[LAST], TO_CORE[2])

    def share(self, m):
        self.got(m, *Y_REST.values())
        self.go(m, TO_CORE[3])
        self.got(m, *X_REST.values())
        self.go(m, TO_CORE[4])

    def end(self, m):
        self.got(m, *TO_CORE)
        for step in range(GATHER_STEPS):
            self.copy(m, step).wait_send()

    def slots(self):
        n = len(self.weights)
        return staged(
            n, ((0, self.spread), (1, self.cross), (2, self.finish), (3, self.share), (4, self.end))
        )

    @staticmethod
    def semaphores(n):
        return [
            pltpu.SemaphoreType.DMA((n, GATHER_STEPS)),
            pltpu.SemaphoreType.DMA((n, GATHER_STEPS)),
            pltpu.SemaphoreType.DMA((n, 2)),
        ]


def whole_shape(kind):
    return {TRIPLE: (3, 1024, 1024), MIXING: (4, 256, 1024), UP: (1024, 4096), DOWN: (4, 1024, 1024)}[kind]


class Turns:
    def start(self):
        for turn in range(2):
            stays, near, far = self.parts(turn)
            pl.when(stays)(near.start)
            pl.when(jnp.logical_not(stays))(far.start)

    def wait(self):
        for turn in range(2):
            stays, near, far = self.parts(turn)
            pl.when(stays)(near.wait)
            pl.when(jnp.logical_not(stays))(far.wait)

    def __init__(self, array, into, send, recv, here):
        self.array, self.into, self.send, self.recv, self.here = array, into, send, recv, here

    @staticmethod
    def semaphores():
        return [pltpu.SemaphoreType.DMA((2,))] * 3


class ToChip(Turns):
    def parts(self, turn):
        t, y, c, x = place()
        slot = lax.rem(turn + t, 2)
        source, into = self.array.at[slot], self.into.at[turn]
        target = (2 * slot + c, y * 2 + t // 2, x)
        stays = jnp.logical_and(2 * slot + c == t, t // 2 == c)
        far = remote(source, into, self.send.at[turn], self.recv.at[turn], target)
        return stays, pltpu.make_async_copy(source, into, self.here.at[turn]), far


class ToOwner(Turns):
    def parts(self, turn):
        t, y, c, x = place()
        owner = 2 * c + lax.rem(t // 2 + turn, 2)
        source, into = self.array.at[turn], self.into.at[lax.rem(turn + owner, 2)]
        stays = jnp.logical_and(owner == t, lax.rem(t, 2) == c)
        far = remote(
            source, into, self.send.at[turn], self.recv.at[turn], (owner, y * 2 + lax.rem(t, 2), x)
        )
        return stays, pltpu.make_async_copy(source, into, self.here.at[turn]), far


ANYWHERE = pl.BlockSpec(memory_space=pl.ANY)
VMEM = pl.BlockSpec(memory_space=pltpu.VMEM)


def gather_kernel(shard, inputs, bias, whole, tokens, biases, *rest):
    t, y, c, x = place()
    gather = Gather([Weight(TRIPLE, shard, whole)], *rest[:3])
    move = ToChip(inputs, tokens, *rest[3:6])
    bias_send, bias_recv, bias_here = rest[6:]
    own_bias = pltpu.make_async_copy(bias, biases.at[t], bias_here.at[0])
    bias_copies = [
        remote(bias, biases.at[t], bias_send.at[k], bias_recv.at[k], (depth_of(q), y * 2 + c, x))
        for k, q in enumerate((NEAR, FAR, LAST))
    ]
    greet(neighbours())
    own_bias.start()
    for copy in bias_copies:
        copy.start()
    gather.begin(0)
    move.start()
    for slot in gather.slots():
        run(slot)
    move.wait()
    own_bias.wait()
    for copy in bias_copies:
        copy.wait()


def gather_first(inputs, bias, shard):
    return pl.pallas_call(
        gather_kernel,
        name="gather_first",
        in_specs=[ANYWHERE] * 3,
        out_specs=[ANYWHERE] * 3,
        out_shape=[
            jax.ShapeDtypeStruct(whole_shape(TRIPLE), bf16),
            jax.ShapeDtypeStruct(inputs.shape, bf16),
            jax.ShapeDtypeStruct((4,) + bias.shape, f32),
        ],
        scratch_shapes=Gather.semaphores(1)
        + Turns.semaphores()
        + [pltpu.SemaphoreType.DMA((3,)), pltpu.SemaphoreType.DMA((3,)), pltpu.SemaphoreType.DMA((1,))],
        compiler_params=pltpu.CompilerParams(collective_id=0, has_side_effects=True),
    )(shard, inputs, bias)


X_FIRST, Y_FIRST0, Y_FIRST1, Y_SECOND, X_SECOND, CORES = range(6)
SUM_STEPS = CORES + 2
Z_LAST, Z_BACK, Z_BESIDE, DONE = range(4)
ORDER = (LAST, FAR, NEAR, OWN)


def shard_shape(kind, rows, lead=()):
    return lead + {TRIPLE: (3, rows, 256), MIXING: (rows, 256), UP: (rows, 1024), DOWN: (4 * rows, 256)}[kind]


def sum_buffers(kind):
    leads = ((256, 4, 2), (256, 4, 2), (48, 4, 2), (80, 4, 2), (48, 4), (80, 4), (128, 3), (128,), (128,))
    return [pltpu.VMEM(shard_shape(kind, rows, tuple(lead)), bf16) for rows, *lead in leads]


BUFFERS = 9


class Total(Weight):
    sections = {HALF: (0, 128), PART_A: (0, 80), PART_B: (80, 48)}

    def __init__(self, kind, part, out, buffers):
        super().__init__(kind, out, part)
        self.acc, self.got_core, self.x1, self.y1, self.y2, self.x2, self.z, self.mine, self.other = buffers

    def sums(self, k, y, part, half):
        r = self.rows(part, half)
        return self.acc.at[k, y, :, r, :] if self.kind == TRIPLE else self.acc.at[k, y, r, :]

    def source(self, k, y, c):
        g = pl.ds(pl.multiple_of((y * 2 + c) * 256, 256), 256)
        t, n = depth_of(ORDER[k]), self.shard.shape[-1]
        if self.kind in (MIXING, DOWN):
            return self.whole.at[t, :, g]
        cols = pl.ds(pl.multiple_of(t * n, n), n)
        return self.whole.at[g, cols] if self.kind == UP else self.whole.at[:, g, cols]


def each(ref, body):
    lead = ref.shape[:-2]
    count = 1
    for n in lead:
        count *= n
    for i in range(count):
        index, rest = [], i
        for n in reversed(lead):
            index.insert(0, rest % n)
            rest //= n

        def step(r, carry, index=tuple(index)):
            body(index + (pl.ds(pl.multiple_of(r * 16, 16), 16),))
            return carry

        lax.fori_loop(0, ref.shape[-2] // 16, step, 0)


def add_into(into, more):
    def body(index):
        into[index] = into[index] + more[index]

    each(more, body)


class Scatter(Copies):
    def __init__(self, totals, send, recv, line_send, line_recv, here):
        self.totals, self.send, self.recv, self.here = totals, send, recv, here
        self.line_send, self.line_recv = line_send, line_recv

    def copy(self, item, step):
        m, k = divmod(item, 4)
        w = self.totals[m]
        _, y, c, x = place()
        if step >= CORES:
            at_y = step - CORES
            source, into, target = w.source(k, at_y, 1 - c), w.got_core.at[k, at_y], CORE
        else:
            source, into, target = {
                X_FIRST: lambda: (w.sums(k, slice(None), PART_B, 1 - x), w.x1.at[k], X),
                Y_FIRST0: lambda: (w.sums(k, 1 - y, PART_A, 0), w.y1.at[k, 0], Y),
                Y_FIRST1: lambda: (w.sums(k, 1 - y, PART_A, 1), w.y1.at[k, 1], Y),
                Y_SECOND: lambda: (w.sums(k, 1 - y, PART_B, x), w.y2.at[k], Y),
                X_SECOND: lambda: (w.sums(k, y, PART_A, 1 - x), w.x2.at[k], X),
            }[step]()
        return remote(source, into, self.send.at[item, step], self.recv.at[item, step], peer(target))

    def line_copy(self, m, step):
        w = self.totals[m]
        _, y, _, x = place()
        source, into, target = {
            Z_LAST: lambda: (w.sums(ORDER.index(LAST), y, HALF, x), w.z.at[0], NEAR),
            Z_BACK: lambda: (w.sums(ORDER.index(FAR), y, HALF, x), w.z.at[1], FAR),
            Z_BESIDE: lambda: (w.sums(ORDER.index(NEAR), y, HALF, x), w.z.at[2], NEAR),
            DONE: lambda: (w.mine, w.other, X),
        }[step]()
        return remote(source, into, self.line_send.at[m, step], self.line_recv.at[m, step], peer(target))

    def load(self, item, y):
        m, k = divmod(item, 4)
        w = self.totals[m]
        return pltpu.make_async_copy(w.source(k, y, place()[2]), w.acc.at[k, y], self.here.at[item, y])

    def begin(self, item):
        for y in range(2):
            self.load(item, y).start()
            self.go(item, CORES + y)

    def cores(self, item):
        m, k = divmod(item, 4)
        for y in range(2):
            self.load(item, y).wait()
            self.got(item, CORES + y)
        add_into(self.totals[m].acc.at[k], self.totals[m].got_core.at[k])
        self.go(item, X_FIRST, Y_FIRST0, Y_FIRST1)

    def second(self, item):
        m, k = divmod(item, 4)
        w = self.totals[m]
        _, y, _, x = place()
        self.got(item, X_FIRST)
        add_into(w.sums(k, slice(None), PART_B, x), w.x1.at[k])
        self.go(item, Y_SECOND)
        self.got(item, Y_FIRST0, Y_FIRST1)
        add_into(w.sums(k, y, PART_A, 0), w.y1.at[k, 0])
        add_into(w.sums(k, y, PART_A, 1), w.y1.at[k, 1])
        self.go(item, X_SECOND)

    def line(self, item):
        m, k = divmod(item, 4)
        w = self.totals[m]
        _, y, _, x = place()
        self.got(item, Y_SECOND)
        add_into(w.sums(k, y, PART_B, x), w.y2.at[k])
        self.got(item, X_SECOND)
        add_into(w.sums(k, y, PART_A, x), w.x2.at[k])
        if ORDER[k] == LAST:
            self.line_copy(m, Z_LAST).start()
        elif ORDER[k] == NEAR:
            self.line_copy(m, Z_BESIDE).start()
        elif ORDER[k] == FAR:
            self.line_copy(m, Z_LAST).wait_recv()
            add_into(w.sums(k, y, HALF, x), w.z.at[0])
            self.line_copy(m, Z_BACK).start()

    def own_half(self, item):
        m, k = divmod(item, 4)
        if ORDER[k] != OWN:
            return
        w = self.totals[m]
        _, y, _, x = place()
        self.line_copy(m, Z_BESIDE).wait_recv()
        self.line_copy(m, Z_BACK).wait_recv()
        own, near, far = w.sums(k, y, HALF, x), w.z.at[2], w.z.at[1]
        out = w.own(HALF, x)

        def body(index):
            total = (own[index].astype(f32) + near[index].astype(f32) + far[index].astype(f32)).astype(bf16)
            w.mine[index] = total
            out[index] = total.astype(f32)

        each(w.mine, body)
        self.line_copy(m, DONE).start()

    def other_half(self, item):
        m, k = divmod(item, 4)
        if ORDER[k] == OWN:
            w = self.totals[m]
            self.line_copy(m, DONE).wait_recv()
            out = w.own(HALF, 1 - place()[3])

            def body(index):
                out[index] = w.other[index].astype(f32)

            each(w.other, body)
            for step in range(4):
                self.line_copy(m, step).wait_send()
        for step in range(SUM_STEPS):
            self.copy(item, step).wait_send()

    def slots(self, lags):
        stages = (self.begin, self.cores, self.second, self.line, self.own_half, self.other_half)
        return staged(4 * len(self.totals), tuple(zip(lags, stages)))

    @staticmethod
    def semaphores(n):
        return [
            pltpu.SemaphoreType.DMA((4 * n, SUM_STEPS)),
            pltpu.SemaphoreType.DMA((4 * n, SUM_STEPS)),
            pltpu.SemaphoreType.DMA((n, 4)),
            pltpu.SemaphoreType.DMA((n, 4)),
            pltpu.SemaphoreType.DMA((4 * n, 2)),
        ]


AROUND = (CORE, X, Y, NEAR, FAR)


def scatter_kernel(kinds, *refs):
    n = len(kinds)
    parts, small, tokens = refs[:n], refs[n], refs[n + 1]
    outs, small_out, slots = refs[n + 2 : 2 * n + 2], refs[2 * n + 2], refs[2 * n + 3]
    rest = refs[2 * n + 4 :]
    buffers, rest = rest[: BUFFERS * n], rest[BUFFERS * n :]
    sums, arrived, small_send, small_recv = rest[:4]
    move = ToOwner(tokens, slots, *rest[4:7])
    scatter = Scatter(
        [Total(kind, parts[i], outs[i], buffers[BUFFERS * i :][:BUFFERS]) for i, kind in enumerate(kinds)],
        *rest[7:],
    )

    def small_copy(k):
        return remote(sums.at[k], arrived.at[k], small_send.at[k], small_recv.at[k], peer(AROUND[k]))

    greet(neighbours())
    move.start()
    sums[0] = small[...]
    small_copy(0).start()
    for k, slot in enumerate(scatter.slots(range(6))):
        run(slot)
        if k < len(AROUND):
            small_copy(k).wait_recv()
            sums[k + 1] = sums[k] + arrived[k]
            if k + 1 < len(AROUND):
                small_copy(k + 1).start()
    small_out[...] = sums[len(AROUND)]
    for k in range(len(AROUND)):
        small_copy(k).wait_send()
    move.wait()


def scatter_last(kinds, parts, small, tokens):
    n = len(kinds)
    scratch = sum((sum_buffers(kind) for kind in kinds), [])
    scratch += [
        pltpu.VMEM((len(AROUND) + 1,) + small.shape, f32),
        pltpu.VMEM((len(AROUND),) + small.shape, f32),
        pltpu.SemaphoreType.DMA((len(AROUND),)),
        pltpu.SemaphoreType.DMA((len(AROUND),)),
    ]
    return pl.pallas_call(
        functools.partial(scatter_kernel, kinds),
        name="scatter_last",
        in_specs=[ANYWHERE] * n + [VMEM, ANYWHERE],
        out_specs=[VMEM] * (n + 1) + [ANYWHERE],
        out_shape=[jax.ShapeDtypeStruct(shard_shape(kind, 256), f32) for kind in kinds]
        + [jax.ShapeDtypeStruct(small.shape, f32), jax.ShapeDtypeStruct(tokens.shape, bf16)],
        scratch_shapes=scratch + Turns.semaphores() + Scatter.semaphores(n),
        compiler_params=pltpu.CompilerParams(
            collective_id=1, has_side_effects=True, vmem_limit_bytes=60 << 20
        ),
    )(*parts, small, tokens)


def at_step(step, slots_at, slots):
    for when in sorted(set(slots_at)):

        @pl.when(step == when)
        def _(when=when):
            for place_at, slot in zip(slots_at, slots):
                if place_at == when:
                    run(slot)


GATHERED = (MIXING, UP, DOWN)
GATHER_AT = (1, 2, 4, 6, 7, 7, 7)
MOVE_AT = 4


def forward_kernel(
    q_ref, ka, va, k_own, v_own, top, s0, s1, s2,
    o_ref, lse_ref, kb, vb, clip_top, w0, w1, w2,
    keys, values_low, values_high, k_far, v_far, pair_send, pair_recv, *rest,
):
    n = ka.shape[0]
    step, last = pl.program_id(0), pl.num_programs(0) - 1
    gather = Gather([Weight(*w) for w in zip(GATHERED, (s0, s1, s2), (w0, w1, w2))], *rest[:3])
    move = ToChip(top, clip_top, *rest[3:6])

    def pair(which, i):
        cols = pl.ds(pl.multiple_of(i * LANES, LANES), LANES)
        own, far = ((k_own, k_far), (v_own, v_far))[which]
        return remote(
            own.at[:, cols], far.at[:, cols], pair_send.at[which, i], pair_recv.at[which, i], peer(CORE)
        )

    @pl.when(step == 0)
    def _():
        greet(neighbours())
        for i in range(k_far.shape[1] // LANES):
            pair(0, i).start()
            pair(1, i).start()
        for m in range(len(GATHERED)):
            gather.begin(m)

    held = (keys, values_low, values_high)
    forward_load(slice(0, n), ka[...], va[...], *held)
    cols = pl.ds(pl.multiple_of(step * LANES, LANES), LANES)
    pair(0, step).wait_recv()
    pair(1, step).wait_recv()
    kb[...], vb[...] = k_far[:, cols], v_far[:, cols]
    forward_load(slice(n, 2 * n), kb[...], vb[...], *held)
    o_ref[...], lse_ref[...] = forward_heads(q_ref[...], *held)

    at_step(step, GATHER_AT, gather.slots())
    pl.when(step == MOVE_AT)(move.start)

    @pl.when(step == last)
    def _():
        for i in range(k_far.shape[1] // LANES):
            pair(0, i).wait_send()
            pair(1, i).wait_send()
        move.wait()


def attend_and_gather(q, k, v, top, shards):
    n, width = q.shape
    spec = pl.BlockSpec((n, LANES), lambda i: (0, i))
    blocks = width // LANES
    return pl.pallas_call(
        forward_kernel,
        grid=(blocks,),
        in_specs=[spec] * 3 + [ANYWHERE] * 6,
        out_specs=[spec] * 4 + [ANYWHERE] * 4,
        out_shape=[jax.ShapeDtypeStruct((n, width), bf16), jax.ShapeDtypeStruct((n, width), f32)]
        + [jax.ShapeDtypeStruct((n, width), bf16)] * 2
        + [jax.ShapeDtypeStruct(top.shape, bf16)]
        + [jax.ShapeDtypeStruct(whole_shape(kind), bf16) for kind in GATHERED],
        scratch_shapes=[pltpu.VMEM((2 * n, LANES), bf16)] * 3
        + [pltpu.VMEM((n, width), bf16)] * 2
        + [pltpu.SemaphoreType.DMA((2, blocks))] * 2
        + Gather.semaphores(len(GATHERED))
        + Turns.semaphores(),
        name="attend_and_gather",
        cost_estimate=pl.CostEstimate(
            flops=8 * n * n * width, bytes_accessed=16 * n * width, transcendentals=n * n * width // 32
        ),
        compiler_params=pltpu.CompilerParams(
            collective_id=2, has_side_effects=True, vmem_limit_bytes=56 << 20
        ),
    )(q, k, v, k, v, top, *shards)


SCATTERED = (DOWN, UP)
SCATTER_AT = (0, 0, 0, 1, 2, 3, 4, 5, 6, 7, 7, 7, 7, 7)


def backward_kernel(
    q_ref, g_ref, o_ref, lse_ref, ka, kb, va, vb, output, p0, p1,
    dq_ref, dk_ref, dv_ref, slots, out0, out1,
    keys, values, dk, dv, far, got, pair_send, pair_recv, *rest,
):
    n = ka.shape[0]
    step, last = pl.program_id(0), pl.num_programs(0) - 1
    buffers, rest = rest[: BUFFERS * 2], rest[BUFFERS * 2 :]
    move = ToOwner(output, slots, *rest[:3])
    scatter = Scatter(
        [Total(DOWN, p0, out0, buffers[:BUFFERS]), Total(UP, p1, out1, buffers[BUFFERS:])], *rest[3:]
    )

    def pair(i):
        return remote(
            far.at[lax.rem(i, 2)], got.at[i], pair_send.at[lax.rem(i, 2)], pair_recv.at[i], peer(CORE)
        )

    @pl.when(step == 0)
    def _():
        greet(neighbours())
        move.start()

    for i, (k, v) in enumerate(((ka, va), (kb, vb))):
        keys[i * n : (i + 1) * n] = k[...]
        values[i * n : (i + 1) * n] = v[...]
    dq_ref[...] = backward_heads(
        q_ref[...], g_ref[...], o_ref[...], lse_ref[...], keys, values, dk, dv
    )

    def settle(i):
        cols = pl.ds(pl.multiple_of(i * LANES, LANES), LANES)
        pair(i).wait_recv()
        dk_ref[:, cols] = (dk_ref[:, cols].astype(f32) + got[i, 0].astype(f32)).astype(bf16)
        dv_ref[:, cols] = (dv_ref[:, cols].astype(f32) + got[i, 1].astype(f32)).astype(bf16)

    key_total, value_total = key_value_total(dk, dv)
    cols = pl.ds(pl.multiple_of(step * LANES, LANES), LANES)
    slot = lax.rem(step, 2)
    dk_ref[:, cols] = key_total[:n].astype(bf16)
    dv_ref[:, cols] = value_total[:n].astype(bf16)

    @pl.when(step >= 2)
    def _():
        pair(step - 2).wait_send()

    far[slot, 0] = key_total[n:].astype(bf16)
    far[slot, 1] = value_total[n:].astype(bf16)
    pair(step).start()

    @pl.when(step >= 1)
    def _():
        settle(step - 1)

    at_step(step, SCATTER_AT, scatter.slots((0, 1, 3, 4, 5, 6)))

    @pl.when(step == last)
    def _():
        settle(last)
        pair(last - 1).wait_send()
        pair(last).wait_send()
        move.wait()


def attend_and_scatter(q, g, o, lse, ka, kb, va, vb, output, parts):
    n, width = q.shape
    spec = pl.BlockSpec((n, LANES), lambda i: (0, i))
    blocks = width // LANES
    return pl.pallas_call(
        backward_kernel,
        grid=(blocks,),
        in_specs=[spec] * 8 + [ANYWHERE] * 3,
        out_specs=[spec] + [VMEM] * 2 + [ANYWHERE] + [VMEM] * 2,
        out_shape=[jax.ShapeDtypeStruct((n, width), bf16)] * 3
        + [jax.ShapeDtypeStruct(output.shape, bf16)]
        + [jax.ShapeDtypeStruct(shard_shape(kind, 256), f32) for kind in SCATTERED],
        scratch_shapes=[pltpu.VMEM((2 * n, LANES), bf16)] * 2
        + [pltpu.VMEM((LANES, 2 * n), f32)] * 2
        + [pltpu.VMEM((2, 2, n, LANES), bf16), pltpu.VMEM((blocks, 2, n, LANES), bf16)]
        + [pltpu.SemaphoreType.DMA((2,)), pltpu.SemaphoreType.DMA((blocks,))]
        + sum_buffers(DOWN)
        + sum_buffers(UP)
        + Turns.semaphores()
        + Scatter.semaphores(len(SCATTERED)),
        name="attend_and_scatter",
        cost_estimate=pl.CostEstimate(
            flops=20 * n * n * width, bytes_accessed=28 * n * width, transcendentals=n * n * width // 32
        ),
        compiler_params=pltpu.CompilerParams(
            collective_id=3, has_side_effects=True, vmem_limit_bytes=62 << 20
        ),
    )(q, g, o, lse, ka, kb, va, vb, output, *parts)


def normalize(values):
    center = values - jnp.mean(values, axis=-1, keepdims=True)
    inverse = lax.rsqrt(jnp.mean(center * center, axis=-1, keepdims=True) + epsilon)
    return (center * inverse, inverse)


def normalize_back(upstream, normed, inverse, norm_gain):
    scaled = upstream * norm_gain
    return inverse * (
        scaled
        - jnp.mean(scaled, axis=-1, keepdims=True)
        - normed * jnp.mean(scaled * normed, axis=-1, keepdims=True)
    )


def clip_exchange(tensor_count, group_count):
    there, back = [], []
    for turn in range(2):
        pairs = []
        for z in range(tensor_count):
            for g in range(group_count):
                slot = (turn + z) % 2
                target = (2 * slot + g % 2) * group_count + g - g % 2 + z // 2
                pairs.append((z * group_count + g, target))
        there.append(pairs)
        back.append([(b, a) for a, b in pairs])
    return there, back


def local(
    inputs,
    clips_here,
    first_gain,
    first_shift,
    query_key_value,
    query_bias,
    value_bias,
    output_weight,
    output_bias,
    second_gain,
    second_shift,
    expand_weight,
    expand_bias,
    contract_weight,
    contract_bias,
    output_grad,
):
    slot_count, rows, width = inputs.shape
    tensor_index = lax.axis_index("tensor")
    tensor_count = lax.axis_size("tensor")
    group_index = lax.axis_index("group")
    group_count = lax.axis_size("group")
    both = ("tensor", "group")
    there, back = clip_exchange(tensor_count, group_count)
    pair = [(g, g + 1 - 2 * (g % 2)) for g in range(group_count)]

    def to_chip(array):
        pieces = []
        for turn in range(2):
            slot = (turn + tensor_index) % 2
            pieces.append(
                lax.ppermute(lax.dynamic_index_in_dim(array, slot, keepdims=False), both, there[turn])
            )
        return jnp.concatenate(pieces, axis=0)

    def to_owner(array):
        received = [
            lax.ppermute(array[turn * rows : (turn + 1) * rows], both, back[turn]) for turn in range(2)
        ]
        even = tensor_index % 2 == 0
        return jnp.stack(
            [jnp.where(even, received[0], received[1]), jnp.where(even, received[1], received[0])]
        )

    def gather(shard):
        return lax.all_gather(shard, both, axis=0).reshape(tensor_count, group_count, *shard.shape)

    direct = (tensor_count, group_count, lax.axis_size("cross")) == (4, 4, 2)
    alive = (jnp.arange(slot_count, dtype=jnp.int32) < clips_here[0]).astype(bf16)[:, None, None]
    bias = jnp.concatenate([query_bias, value_bias, expand_bias])
    if direct:
        bias_size = bias.shape[0]
        bias = jnp.pad(bias.astype(f32), (0, -bias_size % (8 * LANES))).reshape(-1, LANES)
        triple, tokens, biases = gather_first(inputs, bias, query_key_value)
        tokens = tokens.reshape(-1, width).astype(f32)
        biases = biases.reshape(tensor_count, -1)[:, :bias_size]
    else:
        tokens = to_chip(inputs).astype(f32)
        triple = gather(query_key_value).transpose(2, 1, 3, 0, 4).reshape(3, width, width)
        mixing = gather(output_weight).transpose(0, 2, 1, 3).reshape(width, width)
        up = gather(expand_weight).transpose(1, 2, 0, 3).reshape(width, -1)
        down = gather(contract_weight).transpose(0, 2, 1, 3).reshape(-1, width)
        biases = lax.all_gather(bias, "tensor", axis=0).astype(f32)
    split_at = (query_bias.shape[0], query_bias.shape[0] + value_bias.shape[0])
    query_offset, value_offset, hidden_offset = (
        part.reshape(-1) for part in jnp.split(biases, split_at, axis=1)
    )

    gain_one = first_gain.astype(f32)
    gain_two = second_gain.astype(f32)
    first_plain, first_inverse = normalize(tokens)
    first_rows = (first_plain * gain_one + first_shift.astype(f32)).astype(bf16)
    keys = dot(first_rows, triple[1]).astype(bf16)
    values = (dot(first_rows, triple[2]) + value_offset).astype(bf16)
    queries = ((dot(first_rows, triple[0]) + query_offset) * query_scale).astype(bf16)
    if direct:
        attended, log_totals, far_keys, far_values, top, mixing, up, down = attend_and_gather(
            queries, keys, values, output_grad * alive, (output_weight, expand_weight, contract_weight)
        )
        top, mixing, down = top.reshape(-1, width), mixing.reshape(-1, width), down.reshape(-1, width)
    else:
        top = to_chip(output_grad * alive)
        far_keys = lax.ppermute(keys, "group", pair)
        far_values = lax.ppermute(values, "group", pair)
        attended, log_totals = attend_forward(queries, keys, far_keys, values, far_values)
    middle = tokens + dot(attended, mixing) + output_bias.astype(f32)
    second_plain, second_inverse = normalize(middle)
    second_rows = (second_plain * gain_two + second_shift.astype(f32)).astype(bf16)
    hidden_pre = dot(second_rows, up) + hidden_offset
    normal_cdf = 0.5 * (1.0 + lax.erf(hidden_pre * root_half))
    hidden = (hidden_pre * normal_cdf).astype(bf16)
    slope = normal_cdf + hidden_pre * (inv_root_two_pi * jnp.exp(-0.5 * hidden_pre * hidden_pre))
    output = (middle + dot(hidden, down) + contract_bias.astype(f32)).astype(bf16)

    contract_bias_part = jnp.sum(top.astype(f32), axis=0)
    contract_part = dot(hidden, top, TN).astype(bf16)
    pre_grad = (dot(top, down, NT) * slope).astype(bf16)
    expand_bias_part = jnp.sum(pre_grad.astype(f32), axis=0)
    expand_part = dot(second_rows, pre_grad, TN).astype(bf16)
    second_grad = dot(pre_grad, up, NT)
    second_gain_part = jnp.sum(second_grad * second_plain, axis=0)
    second_shift_part = jnp.sum(second_grad, axis=0)
    middle_grad = top.astype(f32) + normalize_back(second_grad, second_plain, second_inverse, gain_two)
    branch_grad = middle_grad.astype(bf16)
    output_bias_part = jnp.sum(branch_grad.astype(f32), axis=0)
    mixing_part = dot(attended, branch_grad, TN).astype(bf16)
    attended_grad = dot(branch_grad, mixing, NT).astype(bf16)
    if direct:
        query_grad, key_grad, value_grad, output, contract_sum, expand_sum = attend_and_scatter(
            queries, attended_grad, attended, log_totals, keys, far_keys, values, far_values,
            output.reshape(inputs.shape), (contract_part.reshape(4, -1, width), expand_part),
        )
    else:
        output = to_owner(output)
        query_grad, key_own, key_far, value_own, value_far = attend_backward(
            queries, attended_grad, attended, log_totals, keys, far_keys, values, far_values
        )
        key_grad = (key_own.astype(f32) + lax.ppermute(key_far, "group", pair).astype(f32)).astype(bf16)
        value_grad = (value_own.astype(f32) + lax.ppermute(value_far, "group", pair).astype(f32)).astype(
            bf16
        )
    query_bias_part = jnp.sum(query_grad.astype(f32), axis=0)
    value_bias_part = jnp.sum(value_grad.astype(f32), axis=0)
    triple_part = jnp.stack(
        [dot(first_rows, d, TN).astype(bf16) for d in (query_grad, key_grad, value_grad)]
    )
    first_grad = (
        dot(query_grad, triple[0], NT) + dot(key_grad, triple[1], NT) + dot(value_grad, triple[2], NT)
    )
    first_gain_part = jnp.sum(first_grad * first_plain, axis=0)
    first_shift_part = jnp.sum(first_grad, axis=0)
    input_grad = (
        middle_grad + normalize_back(first_grad, first_plain, first_inverse, gain_one)
    ).astype(bf16)

    small_parts = (
        first_gain_part,
        first_shift_part,
        query_bias_part,
        value_bias_part,
        output_bias_part,
        second_gain_part,
        second_shift_part,
        expand_bias_part,
        contract_bias_part,
    )
    if direct:
        mixing_sum, triple_sum, small, input_grad = scatter_last(
            (MIXING, TRIPLE),
            (mixing_part.reshape(4, -1, width), triple_part),
            jnp.concatenate(small_parts).reshape(-1, LANES),
            input_grad.reshape(inputs.shape),
        )
        small, small_sums = small.reshape(-1), []
        for part in small_parts:
            small_sums.append(small[: part.shape[0]])
            small = small[part.shape[0] :]
    else:
        input_grad = to_owner(input_grad)

        def scatter(stacked):
            count = tensor_count * group_count
            part = lax.psum_scatter(stacked.reshape(count, *stacked.shape[2:]), both, scatter_dimension=0)
            return lax.psum(part, "cross").astype(f32)

        depth, across = width // group_count, width // tensor_count
        unit = expand_bias.shape[0]
        triple_sum = scatter(
            triple_part.reshape(3, group_count, depth, tensor_count, across).transpose(3, 1, 0, 2, 4)
        )
        mixing_sum = scatter(
            mixing_part.reshape(tensor_count, across, group_count, depth).transpose(0, 2, 1, 3)
        )
        expand_sum = scatter(
            expand_part.reshape(group_count, depth, tensor_count, unit).transpose(2, 0, 1, 3)
        )
        contract_sum = scatter(
            contract_part.reshape(tensor_count, unit, group_count, depth).transpose(0, 2, 1, 3)
        )
        small_sums = lax.psum(small_parts, ("tensor", "group", "cross"))

    def own_group(full_vector):
        size = full_vector.shape[0] // group_count
        return lax.dynamic_slice_in_dim(full_vector, group_index * size, size)

    def own_split(full_vector):
        size = full_vector.shape[0] // (group_count * tensor_count)
        return lax.dynamic_slice_in_dim(
            full_vector, (tensor_index * group_count + group_index) * size, size
        )

    return (
        output,
        input_grad,
        own_group(small_sums[0]),
        own_group(small_sums[1]),
        triple_sum,
        own_split(small_sums[2]),
        own_split(small_sums[3]),
        mixing_sum,
        own_group(small_sums[4]),
        own_group(small_sums[5]),
        own_group(small_sums[6]),
        expand_sum,
        own_split(small_sums[7]),
        contract_sum,
        own_group(small_sums[8]),
    )


def solution(mesh):
    in_specs = (
        P(("group", "cross"), "tensor", None),
        P(("group", "cross")),
        P(),
        P(),
        P(None, "group", "tensor"),
        P("tensor"),
        P("tensor"),
        P("tensor", "group"),
        P(),
        P(),
        P(),
        P("group", "tensor"),
        P("tensor"),
        P("tensor", "group"),
        P(),
        P(("group", "cross"), "tensor", None),
    )
    out_specs = (
        P(("group", "cross"), "tensor", None),
        P(("group", "cross"), "tensor", None),
        P("group"),
        P("group"),
        P(None, "group", "tensor"),
        P(("tensor", "group")),
        P(("tensor", "group")),
        P("tensor", "group"),
        P("group"),
        P("group"),
        P("group"),
        P("group", "tensor"),
        P(("tensor", "group")),
        P("tensor", "group"),
        P("group"),
    )
    return jax.shard_map(local, mesh=mesh, in_specs=in_specs, out_specs=out_specs, check_vma=False)
```

```python
import functools

import jax
import jax.numpy as jnp
from jax import lax
from jax.experimental import pallas as pl
from jax.experimental.pallas import tpu as pltpu
from jax.sharding import PartitionSpec as P

HEAD = 64
LANES = 128

epsilon = 1e-06
root_half = 0.7071067811865476
inv_root_two_pi = 0.3989422804014327
log_two = 0.6931471805599453
query_scale = HEAD**-0.5 / log_two

f32 = jnp.float32
bf16 = jnp.bfloat16

NN = (((1,), (0,)), ((), ()))
NT = (((1,), (1,)), ((), ()))
TN = (((0,), (0,)), ((), ()))


def dot(a, b, dims=NN):
    return lax.dot_general(a, b, dims, preferred_element_type=f32)


def low_lanes(array):
    return lax.broadcasted_iota(jnp.int32, array.shape, 1) < HEAD


def forward_load(rows, k, v, keys, values_low, values_high):
    low, one = low_lanes(v), jnp.ones_like(v)
    keys[rows] = k
    values_low[rows] = jnp.where(low, v, one)
    values_high[rows] = jnp.where(low, one, v)


def forward_heads(q, keys, values_low, values_high):
    low, zero = low_lanes(q), jnp.zeros_like(q)
    sums, tops = [], []
    for mine, v in ((jnp.where(low, q, zero), values_low), (jnp.where(low, zero, q), values_high)):
        s = dot(mine, keys[...], NT)
        top = jnp.max(s, axis=1, keepdims=True)
        p = jnp.exp2(s - top).astype(bf16)
        sums.append(dot(p, v[...]))
        tops.append(top)
    total = pltpu.roll(jnp.where(low, sums[1], sums[0]), HEAD, 1)
    out = (jnp.where(low, sums[0], sums[1]) / total).astype(bf16)
    return out, jnp.where(low, tops[0], tops[1]) + jnp.log2(total)


def backward_heads(q, g, o, lse, keys, values, dk, dv):
    low = low_lanes(q)
    product = g.astype(f32) * o.astype(f32)
    q_t, g_t = q.T, g.T
    dqs = []
    for h in range(2):

        def own(a):
            zero = jnp.zeros_like(a)
            return jnp.where(low, a, zero) if h == 0 else jnp.where(low, zero, a)

        inner = jnp.sum(own(product), axis=1, keepdims=True)
        p = jnp.exp2(dot(own(q), keys[...], NT) - lse[:, HEAD * h : HEAD * h + 1])
        ds = (p * (dot(own(g), values[...], NT) - inner)).astype(bf16)
        dqs.append(dot(ds, keys[...]))
        rows = slice(HEAD * h, HEAD * (h + 1))
        dv[rows] = dot(g_t[rows], p.astype(bf16))
        dk[rows] = dot(q_t[rows], ds)
    return (jnp.where(low, dqs[0], dqs[1]) * HEAD**-0.5).astype(bf16)


def key_value_total(dk, dv):
    return (dk[...] * log_two).T, dv[...].T


def attend_forward_kernel(q_ref, ka, kb, va, vb, o_ref, lse_ref, *held):
    n = ka.shape[0]
    forward_load(slice(0, n), ka[...], va[...], *held)
    forward_load(slice(n, 2 * n), kb[...], vb[...], *held)
    o_ref[...], lse_ref[...] = forward_heads(q_ref[...], *held)


def attend_backward_kernel(
    q_ref, g_ref, o_ref, lse_ref, ka, kb, va, vb,
    dq_ref, dka, dkb, dva, dvb,
    keys, values, dk, dv,
):
    n = ka.shape[0]
    for i, (k, v) in enumerate(((ka, va), (kb, vb))):
        keys[i * n : (i + 1) * n] = k[...]
        values[i * n : (i + 1) * n] = v[...]
    dq_ref[...] = backward_heads(
        q_ref[...], g_ref[...], o_ref[...], lse_ref[...], keys, values, dk, dv
    )
    key_total, value_total = key_value_total(dk, dv)
    dka[...] = key_total[:n].astype(bf16)
    dkb[...] = key_total[n:].astype(bf16)
    dva[...] = value_total[:n].astype(bf16)
    dvb[...] = value_total[n:].astype(bf16)


def attend_forward(q, ka, kb, va, vb):
    n, width = q.shape
    spec = pl.BlockSpec((n, LANES), lambda i: (0, i))
    return pl.pallas_call(
        attend_forward_kernel,
        grid=(width // LANES,),
        in_specs=[spec] * 5,
        out_specs=[spec] * 2,
        out_shape=[jax.ShapeDtypeStruct((n, width), bf16), jax.ShapeDtypeStruct((n, width), f32)],
        scratch_shapes=[pltpu.VMEM((2 * n, LANES), bf16)] * 3,
        name="attend_forward",
        cost_estimate=pl.CostEstimate(
            flops=8 * n * n * width, bytes_accessed=16 * n * width, transcendentals=n * n * width // 32
        ),
        compiler_params=pltpu.CompilerParams(vmem_limit_bytes=56 << 20),
    )(q, ka, kb, va, vb)


def attend_backward(q, g, o, lse, ka, kb, va, vb):
    n, width = q.shape
    spec = pl.BlockSpec((n, LANES), lambda i: (0, i))
    return pl.pallas_call(
        attend_backward_kernel,
        grid=(width // LANES,),
        in_specs=[spec] * 8,
        out_specs=[spec] * 5,
        out_shape=[jax.ShapeDtypeStruct((n, width), bf16)] * 5,
        scratch_shapes=[pltpu.VMEM((2 * n, LANES), bf16)] * 2 + [pltpu.VMEM((LANES, 2 * n), f32)] * 2,
        name="attend_backward",
        cost_estimate=pl.CostEstimate(
            flops=20 * n * n * width, bytes_accessed=28 * n * width, transcendentals=n * n * width // 32
        ),
        compiler_params=pltpu.CompilerParams(vmem_limit_bytes=60 << 20),
    )(q, g, o, lse, ka, kb, va, vb)


MESH = pl.DeviceIdType.MESH
AXES = ("tensor", "group", "cross")
TRIPLE, MIXING, UP, DOWN = range(4)
CORE, X, Y, NEAR, FAR = range(5)
OWN, LAST = 5, 6
HALF, PART_A, PART_B = range(3)


def place():
    t, g, x = (lax.axis_index(axis) for axis in AXES)
    return t, g // 2, g % 2, x


def depth_of(which):
    t = lax.axis_index(AXES[0])
    near = t + 1 - 2 * (t % 2)
    return {OWN: t, NEAR: near, FAR: lax.rem(t + 2, 4), LAST: lax.rem(near + 2, 4)}[which]


def peer(kind):
    t, y, c, x = place()
    if kind in (NEAR, FAR):
        t = depth_of(kind)
    elif kind == X:
        x = 1 - x
    elif kind == Y:
        y = 1 - y
    else:
        c = 1 - c
    return (t, y * 2 + c, x)


def greet(devices):
    barrier = pltpu.get_barrier_semaphore()
    for device in devices:
        pl.semaphore_signal(barrier, inc=1, device_id=device, device_id_type=MESH)
    pl.semaphore_wait(barrier, len(devices))


def remote(source, target, send, recv, device):
    return pltpu.make_async_remote_copy(
        source, target, send, recv, device_id=device, device_id_type=MESH
    )


def chip_line():
    t, y, c, x = place()
    devices = [(t, y * 2 + 1 - c, x)]
    for step in range(1, 4):
        for core in range(2):
            devices.append((lax.rem(t + step, 4), y * 2 + core, x))
    return devices


def neighbours():
    return chip_line() + [peer(X), peer(Y)]


def staged(count, stages):
    slots = []
    for now in range(count + max(delay for delay, _ in stages)):
        slots.append(
            [(stage, now - delay) for delay, stage in stages if 0 <= now - delay < count]
        )
    return slots


def run(slot):
    for stage, item in slot:
        stage(item)


class Copies:
    def go(self, m, *steps):
        for step in steps:
            self.copy(m, step).start()

    def got(self, m, *steps):
        for step in steps:
            self.copy(m, step).wait_recv()


class Weight:
    sections = {HALF: (0, 128), PART_A: (0, 48), PART_B: (48, 80)}

    def __init__(self, kind, shard, whole):
        self.kind, self.shard, self.whole = kind, shard, whole
        self.unit = 4 if kind == DOWN else 1

    def rows(self, part, half, base=0):
        off, size = self.sections[part]
        return pl.ds(pl.multiple_of(base + (half * 128 + off) * self.unit, 16), size * self.unit)

    def own(self, part, half):
        r = self.rows(part, half)
        return self.shard.at[:, r, :] if self.kind == TRIPLE else self.shard.at[r, :]

    def at(self, y, c, part, half, depth=None):
        g = y * 2 + c
        if self.kind in (TRIPLE, UP):
            n = self.shard.shape[-1]
            r = self.rows(part, half, g * 256)
            cols = slice(None) if depth is None else pl.ds(pl.multiple_of(depth * n, n), n)
            return self.whole.at[:, r, cols] if self.kind == TRIPLE else self.whole.at[r, cols]
        cols = pl.ds(pl.multiple_of(g * 256, 256), 256)
        return self.whole.at[slice(None) if depth is None else depth, self.rows(part, half), cols]


Z_NEAR, Z_FAR, Z_ON = 0, 1, 2
X_HALF = {NEAR: 3, FAR: 4, LAST: 5}
Y_HALF = {OWN: 6, NEAR: 7, FAR: 8, LAST: 9}
Y_REST = {OWN: 10, NEAR: 11, FAR: 12, LAST: 13}
X_REST = {OWN: 14, NEAR: 15, FAR: 16, LAST: 17}
TO_CORE = (18, 19, 20, 21, 22)
GATHER_STEPS = 23


class Gather(Copies):
    def __init__(self, weights, send, recv, here):
        self.weights, self.send, self.recv, self.here = weights, send, recv, here

    def copy(self, m, step):
        w = self.weights[m]
        t, y, c, x = place()
        if step in (Z_NEAR, Z_FAR):
            target = NEAR if step == Z_NEAR else FAR
            source, into = w.own(HALF, x), w.at(y, c, HALF, x, t)
        elif step == Z_ON:
            target = NEAR
            source = into = w.at(y, c, HALF, x, depth_of(FAR))
        elif step in TO_CORE:
            target = CORE
            at_y, part, half = (
                (y, HALF, x),
                (y, HALF, 1 - x),
                (1 - y, HALF, x),
                (1 - y, PART_A, 1 - x),
                (1 - y, PART_B, 1 - x),
            )[step - TO_CORE[0]]
            source = into = w.at(at_y, c, part, half)
        else:
            for steps, target, at_y, part, half in (
                (X_HALF, X, y, HALF, x),
                (Y_HALF, Y, y, HALF, x),
                (Y_REST, Y, y, PART_A, 1 - x),
                (X_REST, X, 1 - y, PART_B, x),
            ):
                depths = [which for which, k in steps.items() if k == step]
                if depths:
                    break
            source = into = w.at(at_y, c, part, half, depth_of(depths[0]))
            if step in (Y_HALF[OWN], Y_REST[OWN]):
                source = w.own(part, half)
        return remote(source, into, self.send.at[m, step], self.recv.at[m, step], peer(target))

    def own_copy(self, m, half):
        t, y, c, _ = place()
        w = self.weights[m]
        return pltpu.make_async_copy(w.own(HALF, half), w.at(y, c, HALF, half, t), self.here.at[m, half])

    def begin(self, m):
        for half in range(2):
            self.own_copy(m, half).start()
        self.go(m, Z_FAR, Z_NEAR, Y_HALF[OWN], Y_REST[OWN])

    def spread(self, m):
        self.got(m, Z_FAR)
        self.go(m, Z_ON, X_HALF[FAR], Y_HALF[FAR])
        self.got(m, Z_NEAR)
        self.go(m, X_HALF[NEAR], Y_HALF[NEAR])
        self.got(m, Y_HALF[OWN])
        self.go(m, X_REST[OWN])

    def cross(self, m):
        self.got(m, Z_ON)
        self.go(m, X_HALF[LAST], Y_HALF[LAST])
        for half in range(2):
            self.own_copy(m, half).wait()
        self.go(m, TO_CORE[0])
        for q in (FAR, NEAR):
            self.got(m, X_HALF[q])
            self.go(m, Y_REST[q])
            self.got(m, Y_HALF[q])
            self.go(m, X_REST[q])

    def finish(self, m):
        self.got(m, X_HALF[LAST])
        self.go(m, Y_REST[LAST], TO_CORE[1])
        self.got(m, Y_HALF[LAST])
        self.go(m, X_REST[LAST], TO_CORE[2])

    def share(self, m):
        self.got(m, *Y_REST.values())
        self.go(m, TO_CORE[3])
        self.got(m, *X_REST.values())
        self.go(m, TO_CORE[4])

    def end(self, m):
        self.got(m, *TO_CORE)
        for step in range(GATHER_STEPS):
            self.copy(m, step).wait_send()

    def slots(self):
        n = len(self.weights)
        return staged(
            n, ((0, self.spread), (1, self.cross), (2, self.finish), (3, self.share), (4, self.end))
        )

    @staticmethod
    def semaphores(n):
        return [
            pltpu.SemaphoreType.DMA((n, GATHER_STEPS)),
            pltpu.SemaphoreType.DMA((n, GATHER_STEPS)),
            pltpu.SemaphoreType.DMA((n, 2)),
        ]


def whole_shape(kind):
    return {TRIPLE: (3, 1024, 1024), MIXING: (4, 256, 1024), UP: (1024, 4096), DOWN: (4, 1024, 1024)}[kind]


class Turns:
    def start(self):
        for turn in range(2):
            stays, near, far = self.parts(turn)
            pl.when(stays)(near.start)
            pl.when(jnp.logical_not(stays))(far.start)

    def wait(self):
        for turn in range(2):
            stays, near, far = self.parts(turn)
            pl.when(stays)(near.wait)
            pl.when(jnp.logical_not(stays))(far.wait)

    def __init__(self, array, into, send, recv, here):
        self.array, self.into, self.send, self.recv, self.here = array, into, send, recv, here

    @staticmethod
    def semaphores():
        return [pltpu.SemaphoreType.DMA((2,))] * 3


class ToChip(Turns):
    def parts(self, turn):
        t, y, c, x = place()
        slot = lax.rem(turn + t, 2)
        source, into = self.array.at[slot], self.into.at[turn]
        target = (2 * slot + c, y * 2 + t // 2, x)
        stays = jnp.logical_and(2 * slot + c == t, t // 2 == c)
        far = remote(source, into, self.send.at[turn], self.recv.at[turn], target)
        return stays, pltpu.make_async_copy(source, into, self.here.at[turn]), far


class ToOwner(Turns):
    def parts(self, turn):
        t, y, c, x = place()
        owner = 2 * c + lax.rem(t // 2 + turn, 2)
        source, into = self.array.at[turn], self.into.at[lax.rem(turn + owner, 2)]
        stays = jnp.logical_and(owner == t, lax.rem(t, 2) == c)
        far = remote(
            source, into, self.send.at[turn], self.recv.at[turn], (owner, y * 2 + lax.rem(t, 2), x)
        )
        return stays, pltpu.make_async_copy(source, into, self.here.at[turn]), far


ANYWHERE = pl.BlockSpec(memory_space=pl.ANY)
VMEM = pl.BlockSpec(memory_space=pltpu.VMEM)


def gather_kernel(shard, inputs, bias, whole, tokens, biases, *rest):
    t, y, c, x = place()
    gather = Gather([Weight(TRIPLE, shard, whole)], *rest[:3])
    move = ToChip(inputs, tokens, *rest[3:6])
    bias_send, bias_recv, bias_here = rest[6:]
    own_bias = pltpu.make_async_copy(bias, biases.at[t], bias_here.at[0])
    bias_copies = [
        remote(bias, biases.at[t], bias_send.at[k], bias_recv.at[k], (depth_of(q), y * 2 + c, x))
        for k, q in enumerate((NEAR, FAR, LAST))
    ]
    greet(neighbours())
    own_bias.start()
    for copy in bias_copies:
        copy.start()
    gather.begin(0)
    move.start()
    for slot in gather.slots():
        run(slot)
    move.wait()
    own_bias.wait()
    for copy in bias_copies:
        copy.wait()


def gather_first(inputs, bias, shard):
    return pl.pallas_call(
        gather_kernel,
        name="gather_first",
        in_specs=[ANYWHERE] * 3,
        out_specs=[ANYWHERE] * 3,
        out_shape=[
            jax.ShapeDtypeStruct(whole_shape(TRIPLE), bf16),
            jax.ShapeDtypeStruct(inputs.shape, bf16),
            jax.ShapeDtypeStruct((4,) + bias.shape, f32),
        ],
        scratch_shapes=Gather.semaphores(1)
        + Turns.semaphores()
        + [pltpu.SemaphoreType.DMA((3,)), pltpu.SemaphoreType.DMA((3,)), pltpu.SemaphoreType.DMA((1,))],
        compiler_params=pltpu.CompilerParams(collective_id=0, has_side_effects=True),
    )(shard, inputs, bias)


X_FIRST, Y_FIRST0, Y_FIRST1, Y_SECOND, X_SECOND, CORES = range(6)
SUM_STEPS = CORES + 2
Z_LAST, Z_BACK, Z_BESIDE, DONE = range(4)
ORDER = (LAST, FAR, NEAR, OWN)


def shard_shape(kind, rows, lead=()):
    return lead + {TRIPLE: (3, rows, 256), MIXING: (rows, 256), UP: (rows, 1024), DOWN: (4 * rows, 256)}[kind]


def sum_buffers(kind):
    leads = ((256, 4, 2), (256, 4, 2), (48, 4, 2), (80, 4, 2), (48, 4), (80, 4), (128, 3), (128,), (128,))
    return [pltpu.VMEM(shard_shape(kind, rows, tuple(lead)), bf16) for rows, *lead in leads]


BUFFERS = 9


class Total(Weight):
    sections = {HALF: (0, 128), PART_A: (0, 80), PART_B: (80, 48)}

    def __init__(self, kind, part, out, buffers):
        super().__init__(kind, out, part)
        self.acc, self.got_core, self.x1, self.y1, self.y2, self.x2, self.z, self.mine, self.other = buffers

    def sums(self, k, y, part, half):
        r = self.rows(part, half)
        return self.acc.at[k, y, :, r, :] if self.kind == TRIPLE else self.acc.at[k, y, r, :]

    def source(self, k, y, c):
        g = pl.ds(pl.multiple_of((y * 2 + c) * 256, 256), 256)
        t, n = depth_of(ORDER[k]), self.shard.shape[-1]
        if self.kind in (MIXING, DOWN):
            return self.whole.at[t, :, g]
        cols = pl.ds(pl.multiple_of(t * n, n), n)
        return self.whole.at[g, cols] if self.kind == UP else self.whole.at[:, g, cols]


def each(ref, body):
    lead = ref.shape[:-2]
    count = 1
    for n in lead:
        count *= n
    for i in range(count):
        index, rest = [], i
        for n in reversed(lead):
            index.insert(0, rest % n)
            rest //= n

        def step(r, carry, index=tuple(index)):
            body(index + (pl.ds(pl.multiple_of(r * 16, 16), 16),))
            return carry

        lax.fori_loop(0, ref.shape[-2] // 16, step, 0)


def add_into(into, more):
    def body(index):
        into[index] = into[index] + more[index]

    each(more, body)


class Scatter(Copies):
    def __init__(self, totals, send, recv, line_send, line_recv, here):
        self.totals, self.send, self.recv, self.here = totals, send, recv, here
        self.line_send, self.line_recv = line_send, line_recv

    def copy(self, item, step):
        m, k = divmod(item, 4)
        w = self.totals[m]
        _, y, c, x = place()
        if step >= CORES:
            at_y = step - CORES
            source, into, target = w.source(k, at_y, 1 - c), w.got_core.at[k, at_y], CORE
        else:
            source, into, target = {
                X_FIRST: lambda: (w.sums(k, slice(None), PART_B, 1 - x), w.x1.at[k], X),
                Y_FIRST0: lambda: (w.sums(k, 1 - y, PART_A, 0), w.y1.at[k, 0], Y),
                Y_FIRST1: lambda: (w.sums(k, 1 - y, PART_A, 1), w.y1.at[k, 1], Y),
                Y_SECOND: lambda: (w.sums(k, 1 - y, PART_B, x), w.y2.at[k], Y),
                X_SECOND: lambda: (w.sums(k, y, PART_A, 1 - x), w.x2.at[k], X),
            }[step]()
        return remote(source, into, self.send.at[item, step], self.recv.at[item, step], peer(target))

    def line_copy(self, m, step):
        w = self.totals[m]
        _, y, _, x = place()
        source, into, target = {
            Z_LAST: lambda: (w.sums(ORDER.index(LAST), y, HALF, x), w.z.at[0], NEAR),
            Z_BACK: lambda: (w.sums(ORDER.index(FAR), y, HALF, x), w.z.at[1], FAR),
            Z_BESIDE: lambda: (w.sums(ORDER.index(NEAR), y, HALF, x), w.z.at[2], NEAR),
            DONE: lambda: (w.mine, w.other, X),
        }[step]()
        return remote(source, into, self.line_send.at[m, step], self.line_recv.at[m, step], peer(target))

    def load(self, item, y):
        m, k = divmod(item, 4)
        w = self.totals[m]
        return pltpu.make_async_copy(w.source(k, y, place()[2]), w.acc.at[k, y], self.here.at[item, y])

    def begin(self, item):
        for y in range(2):
            self.load(item, y).start()
            self.go(item, CORES + y)

    def cores(self, item):
        m, k = divmod(item, 4)
        for y in range(2):
            self.load(item, y).wait()
            self.got(item, CORES + y)
        add_into(self.totals[m].acc.at[k], self.totals[m].got_core.at[k])
        self.go(item, X_FIRST, Y_FIRST0, Y_FIRST1)

    def second(self, item):
        m, k = divmod(item, 4)
        w = self.totals[m]
        _, y, _, x = place()
        self.got(item, X_FIRST)
        add_into(w.sums(k, slice(None), PART_B, x), w.x1.at[k])
        self.go(item, Y_SECOND)
        self.got(item, Y_FIRST0, Y_FIRST1)
        add_into(w.sums(k, y, PART_A, 0), w.y1.at[k, 0])
        add_into(w.sums(k, y, PART_A, 1), w.y1.at[k, 1])
        self.go(item, X_SECOND)

    def line(self, item):
        m, k = divmod(item, 4)
        w = self.totals[m]
        _, y, _, x = place()
        self.got(item, Y_SECOND)
        add_into(w.sums(k, y, PART_B, x), w.y2.at[k])
        self.got(item, X_SECOND)
        add_into(w.sums(k, y, PART_A, x), w.x2.at[k])
        if ORDER[k] == LAST:
            self.line_copy(m, Z_LAST).start()
        elif ORDER[k] == NEAR:
            self.line_copy(m, Z_BESIDE).start()
        elif ORDER[k] == FAR:
            self.line_copy(m, Z_LAST).wait_recv()
            add_into(w.sums(k, y, HALF, x), w.z.at[0])
            self.line_copy(m, Z_BACK).start()

    def own_half(self, item):
        m, k = divmod(item, 4)
        if ORDER[k] != OWN:
            return
        w = self.totals[m]
        _, y, _, x = place()
        self.line_copy(m, Z_BESIDE).wait_recv()
        self.line_copy(m, Z_BACK).wait_recv()
        own, near, far = w.sums(k, y, HALF, x), w.z.at[2], w.z.at[1]
        out = w.own(HALF, x)

        def body(index):
            total = (own[index].astype(f32) + near[index].astype(f32) + far[index].astype(f32)).astype(bf16)
            w.mine[index] = total
            out[index] = total.astype(f32)

        each(w.mine, body)
        self.line_copy(m, DONE).start()

    def other_half(self, item):
        m, k = divmod(item, 4)
        if ORDER[k] == OWN:
            w = self.totals[m]
            self.line_copy(m, DONE).wait_recv()
            out = w.own(HALF, 1 - place()[3])

            def body(index):
                out[index] = w.other[index].astype(f32)

            each(w.other, body)
            for step in range(4):
                self.line_copy(m, step).wait_send()
        for step in range(SUM_STEPS):
            self.copy(item, step).wait_send()

    def slots(self, lags):
        stages = (self.begin, self.cores, self.second, self.line, self.own_half, self.other_half)
        return staged(4 * len(self.totals), tuple(zip(lags, stages)))

    @staticmethod
    def semaphores(n):
        return [
            pltpu.SemaphoreType.DMA((4 * n, SUM_STEPS)),
            pltpu.SemaphoreType.DMA((4 * n, SUM_STEPS)),
            pltpu.SemaphoreType.DMA((n, 4)),
            pltpu.SemaphoreType.DMA((n, 4)),
            pltpu.SemaphoreType.DMA((4 * n, 2)),
        ]


AROUND = (CORE, X, Y, NEAR, FAR)


def scatter_kernel(kinds, *refs):
    n = len(kinds)
    parts, small, tokens = refs[:n], refs[n], refs[n + 1]
    outs, small_out, slots = refs[n + 2 : 2 * n + 2], refs[2 * n + 2], refs[2 * n + 3]
    rest = refs[2 * n + 4 :]
    buffers, rest = rest[: BUFFERS * n], rest[BUFFERS * n :]
    sums, arrived, small_send, small_recv = rest[:4]
    move = ToOwner(tokens, slots, *rest[4:7])
    scatter = Scatter(
        [Total(kind, parts[i], outs[i], buffers[BUFFERS * i :][:BUFFERS]) for i, kind in enumerate(kinds)],
        *rest[7:],
    )

    def small_copy(k):
        return remote(sums.at[k], arrived.at[k], small_send.at[k], small_recv.at[k], peer(AROUND[k]))

    greet(neighbours())
    move.start()
    sums[0] = small[...]
    small_copy(0).start()
    for k, slot in enumerate(scatter.slots(range(6))):
        run(slot)
        if k < len(AROUND):
            small_copy(k).wait_recv()
            sums[k + 1] = sums[k] + arrived[k]
            if k + 1 < len(AROUND):
                small_copy(k + 1).start()
    small_out[...] = sums[len(AROUND)]
    for k in range(len(AROUND)):
        small_copy(k).wait_send()
    move.wait()


def scatter_last(kinds, parts, small, tokens):
    n = len(kinds)
    scratch = sum((sum_buffers(kind) for kind in kinds), [])
    scratch += [
        pltpu.VMEM((len(AROUND) + 1,) + small.shape, f32),
        pltpu.VMEM((len(AROUND),) + small.shape, f32),
        pltpu.SemaphoreType.DMA((len(AROUND),)),
        pltpu.SemaphoreType.DMA((len(AROUND),)),
    ]
    return pl.pallas_call(
        functools.partial(scatter_kernel, kinds),
        name="scatter_last",
        in_specs=[ANYWHERE] * n + [VMEM, ANYWHERE],
        out_specs=[VMEM] * (n + 1) + [ANYWHERE],
        out_shape=[jax.ShapeDtypeStruct(shard_shape(kind, 256), f32) for kind in kinds]
        + [jax.ShapeDtypeStruct(small.shape, f32), jax.ShapeDtypeStruct(tokens.shape, bf16)],
        scratch_shapes=scratch + Turns.semaphores() + Scatter.semaphores(n),
        compiler_params=pltpu.CompilerParams(
            collective_id=1, has_side_effects=True, vmem_limit_bytes=60 << 20
        ),
    )(*parts, small, tokens)


def at_step(step, slots_at, slots):
    for when in sorted(set(slots_at)):

        @pl.when(step == when)
        def _(when=when):
            for place_at, slot in zip(slots_at, slots):
                if place_at == when:
                    run(slot)


GATHERED = (MIXING, UP, DOWN)
GATHER_AT = (1, 2, 4, 6, 7, 7, 7)
MOVE_AT = 4


def forward_kernel(
    q_ref, ka, va, k_own, v_own, top, s0, s1, s2,
    o_ref, lse_ref, kb, vb, clip_top, w0, w1, w2,
    keys, values_low, values_high, k_far, v_far, pair_send, pair_recv, *rest,
):
    n = ka.shape[0]
    step, last = pl.program_id(0), pl.num_programs(0) - 1
    gather = Gather([Weight(*w) for w in zip(GATHERED, (s0, s1, s2), (w0, w1, w2))], *rest[:3])
    move = ToChip(top, clip_top, *rest[3:6])

    def pair(which, i):
        cols = pl.ds(pl.multiple_of(i * LANES, LANES), LANES)
        own, far = ((k_own, k_far), (v_own, v_far))[which]
        return remote(
            own.at[:, cols], far.at[:, cols], pair_send.at[which, i], pair_recv.at[which, i], peer(CORE)
        )

    @pl.when(step == 0)
    def _():
        greet(neighbours())
        for i in range(k_far.shape[1] // LANES):
            pair(0, i).start()
            pair(1, i).start()
        for m in range(len(GATHERED)):
            gather.begin(m)

    held = (keys, values_low, values_high)
    forward_load(slice(0, n), ka[...], va[...], *held)
    cols = pl.ds(pl.multiple_of(step * LANES, LANES), LANES)
    pair(0, step).wait_recv()
    pair(1, step).wait_recv()
    kb[...], vb[...] = k_far[:, cols], v_far[:, cols]
    forward_load(slice(n, 2 * n), kb[...], vb[...], *held)
    o_ref[...], lse_ref[...] = forward_heads(q_ref[...], *held)

    at_step(step, GATHER_AT, gather.slots())
    pl.when(step == MOVE_AT)(move.start)

    @pl.when(step == last)
    def _():
        for i in range(k_far.shape[1] // LANES):
            pair(0, i).wait_send()
            pair(1, i).wait_send()
        move.wait()


def attend_and_gather(q, k, v, top, shards):
    n, width = q.shape
    spec = pl.BlockSpec((n, LANES), lambda i: (0, i))
    blocks = width // LANES
    return pl.pallas_call(
        forward_kernel,
        grid=(blocks,),
        in_specs=[spec] * 3 + [ANYWHERE] * 6,
        out_specs=[spec] * 4 + [ANYWHERE] * 4,
        out_shape=[jax.ShapeDtypeStruct((n, width), bf16), jax.ShapeDtypeStruct((n, width), f32)]
        + [jax.ShapeDtypeStruct((n, width), bf16)] * 2
        + [jax.ShapeDtypeStruct(top.shape, bf16)]
        + [jax.ShapeDtypeStruct(whole_shape(kind), bf16) for kind in GATHERED],
        scratch_shapes=[pltpu.VMEM((2 * n, LANES), bf16)] * 3
        + [pltpu.VMEM((n, width), bf16)] * 2
        + [pltpu.SemaphoreType.DMA((2, blocks))] * 2
        + Gather.semaphores(len(GATHERED))
        + Turns.semaphores(),
        name="attend_and_gather",
        cost_estimate=pl.CostEstimate(
            flops=8 * n * n * width, bytes_accessed=16 * n * width, transcendentals=n * n * width // 32
        ),
        compiler_params=pltpu.CompilerParams(
            collective_id=2, has_side_effects=True, vmem_limit_bytes=56 << 20
        ),
    )(q, k, v, k, v, top, *shards)


SCATTERED = (DOWN, UP)
SCATTER_AT = (0, 0, 0, 1, 2, 3, 4, 5, 6, 7, 7, 7, 7, 7)


def backward_kernel(
    q_ref, g_ref, o_ref, lse_ref, ka, kb, va, vb, output, p0, p1,
    dq_ref, dk_ref, dv_ref, slots, out0, out1,
    keys, values, dk, dv, far, got, pair_send, pair_recv, *rest,
):
    n = ka.shape[0]
    step, last = pl.program_id(0), pl.num_programs(0) - 1
    buffers, rest = rest[: BUFFERS * 2], rest[BUFFERS * 2 :]
    move = ToOwner(output, slots, *rest[:3])
    scatter = Scatter(
        [Total(DOWN, p0, out0, buffers[:BUFFERS]), Total(UP, p1, out1, buffers[BUFFERS:])], *rest[3:]
    )

    def pair(i):
        return remote(
            far.at[lax.rem(i, 2)], got.at[i], pair_send.at[lax.rem(i, 2)], pair_recv.at[i], peer(CORE)
        )

    @pl.when(step == 0)
    def _():
        greet(neighbours())
        move.start()

    for i, (k, v) in enumerate(((ka, va), (kb, vb))):
        keys[i * n : (i + 1) * n] = k[...]
        values[i * n : (i + 1) * n] = v[...]
    dq_ref[...] = backward_heads(
        q_ref[...], g_ref[...], o_ref[...], lse_ref[...], keys, values, dk, dv
    )

    def settle(i):
        cols = pl.ds(pl.multiple_of(i * LANES, LANES), LANES)
        pair(i).wait_recv()
        dk_ref[:, cols] = (dk_ref[:, cols].astype(f32) + got[i, 0].astype(f32)).astype(bf16)
        dv_ref[:, cols] = (dv_ref[:, cols].astype(f32) + got[i, 1].astype(f32)).astype(bf16)

    key_total, value_total = key_value_total(dk, dv)
    cols = pl.ds(pl.multiple_of(step * LANES, LANES), LANES)
    slot = lax.rem(step, 2)
    dk_ref[:, cols] = key_total[:n].astype(bf16)
    dv_ref[:, cols] = value_total[:n].astype(bf16)

    @pl.when(step >= 2)
    def _():
        pair(step - 2).wait_send()

    far[slot, 0] = key_total[n:].astype(bf16)
    far[slot, 1] = value_total[n:].astype(bf16)
    pair(step).start()

    @pl.when(step >= 1)
    def _():
        settle(step - 1)

    at_step(step, SCATTER_AT, scatter.slots((0, 1, 3, 4, 5, 6)))

    @pl.when(step == last)
    def _():
        settle(last)
        pair(last - 1).wait_send()
        pair(last).wait_send()
        move.wait()


def attend_and_scatter(q, g, o, lse, ka, kb, va, vb, output, parts):
    n, width = q.shape
    spec = pl.BlockSpec((n, LANES), lambda i: (0, i))
    blocks = width // LANES
    return pl.pallas_call(
        backward_kernel,
        grid=(blocks,),
        in_specs=[spec] * 8 + [ANYWHERE] * 3,
        out_specs=[spec] + [VMEM] * 2 + [ANYWHERE] + [VMEM] * 2,
        out_shape=[jax.ShapeDtypeStruct((n, width), bf16)] * 3
        + [jax.ShapeDtypeStruct(output.shape, bf16)]
        + [jax.ShapeDtypeStruct(shard_shape(kind, 256), f32) for kind in SCATTERED],
        scratch_shapes=[pltpu.VMEM((2 * n, LANES), bf16)] * 2
        + [pltpu.VMEM((LANES, 2 * n), f32)] * 2
        + [pltpu.VMEM((2, 2, n, LANES), bf16), pltpu.VMEM((blocks, 2, n, LANES), bf16)]
        + [pltpu.SemaphoreType.DMA((2,)), pltpu.SemaphoreType.DMA((blocks,))]
        + sum_buffers(DOWN)
        + sum_buffers(UP)
        + Turns.semaphores()
        + Scatter.semaphores(len(SCATTERED)),
        name="attend_and_scatter",
        cost_estimate=pl.CostEstimate(
            flops=20 * n * n * width, bytes_accessed=28 * n * width, transcendentals=n * n * width // 32
        ),
        compiler_params=pltpu.CompilerParams(
            collective_id=3, has_side_effects=True, vmem_limit_bytes=62 << 20
        ),
    )(q, g, o, lse, ka, kb, va, vb, output, *parts)


def normalize(values):
    center = values - jnp.mean(values, axis=-1, keepdims=True)
    inverse = lax.rsqrt(jnp.mean(center * center, axis=-1, keepdims=True) + epsilon)
    return (center * inverse, inverse)


def normalize_back(upstream, normed, inverse, norm_gain):
    scaled = upstream * norm_gain
    return inverse * (
        scaled
        - jnp.mean(scaled, axis=-1, keepdims=True)
        - normed * jnp.mean(scaled * normed, axis=-1, keepdims=True)
    )


def clip_exchange(tensor_count, group_count):
    there, back = [], []
    for turn in range(2):
        pairs = []
        for z in range(tensor_count):
            for g in range(group_count):
                slot = (turn + z) % 2
                target = (2 * slot + g % 2) * group_count + g - g % 2 + z // 2
                pairs.append((z * group_count + g, target))
        there.append(pairs)
        back.append([(b, a) for a, b in pairs])
    return there, back


def local(
    inputs,
    clips_here,
    first_gain,
    first_shift,
    query_key_value,
    query_bias,
    value_bias,
    output_weight,
    output_bias,
    second_gain,
    second_shift,
    expand_weight,
    expand_bias,
    contract_weight,
    contract_bias,
    output_grad,
):
    slot_count, rows, width = inputs.shape
    tensor_index = lax.axis_index("tensor")
    tensor_count = lax.axis_size("tensor")
    group_index = lax.axis_index("group")
    group_count = lax.axis_size("group")
    both = ("tensor", "group")
    there, back = clip_exchange(tensor_count, group_count)
    pair = [(g, g + 1 - 2 * (g % 2)) for g in range(group_count)]

    def to_chip(array):
        pieces = []
        for turn in range(2):
            slot = (turn + tensor_index) % 2
            pieces.append(
                lax.ppermute(lax.dynamic_index_in_dim(array, slot, keepdims=False), both, there[turn])
            )
        return jnp.concatenate(pieces, axis=0)

    def to_owner(array):
        received = [
            lax.ppermute(array[turn * rows : (turn + 1) * rows], both, back[turn]) for turn in range(2)
        ]
        even = tensor_index % 2 == 0
        return jnp.stack(
            [jnp.where(even, received[0], received[1]), jnp.where(even, received[1], received[0])]
        )

    def gather(shard):
        return lax.all_gather(shard, both, axis=0).reshape(tensor_count, group_count, *shard.shape)

    direct = (tensor_count, group_count, lax.axis_size("cross")) == (4, 4, 2)
    alive = (jnp.arange(slot_count, dtype=jnp.int32) < clips_here[0]).astype(bf16)[:, None, None]
    bias = jnp.concatenate([query_bias, value_bias, expand_bias])
    if direct:
        bias_size = bias.shape[0]
        bias = jnp.pad(bias.astype(f32), (0, -bias_size % (8 * LANES))).reshape(-1, LANES)
        triple, tokens, biases = gather_first(inputs, bias, query_key_value)
        tokens = tokens.reshape(-1, width).astype(f32)
        biases = biases.reshape(tensor_count, -1)[:, :bias_size]
    else:
        tokens = to_chip(inputs).astype(f32)
        triple = gather(query_key_value).transpose(2, 1, 3, 0, 4).reshape(3, width, width)
        mixing = gather(output_weight).transpose(0, 2, 1, 3).reshape(width, width)
        up = gather(expand_weight).transpose(1, 2, 0, 3).reshape(width, -1)
        down = gather(contract_weight).transpose(0, 2, 1, 3).reshape(-1, width)
        biases = lax.all_gather(bias, "tensor", axis=0).astype(f32)
    split_at = (query_bias.shape[0], query_bias.shape[0] + value_bias.shape[0])
    query_offset, value_offset, hidden_offset = (
        part.reshape(-1) for part in jnp.split(biases, split_at, axis=1)
    )

    gain_one = first_gain.astype(f32)
    gain_two = second_gain.astype(f32)
    first_plain, first_inverse = normalize(tokens)
    first_rows = (first_plain * gain_one + first_shift.astype(f32)).astype(bf16)
    keys = dot(first_rows, triple[1]).astype(bf16)
    values = (dot(first_rows, triple[2]) + value_offset).astype(bf16)
    queries = ((dot(first_rows, triple[0]) + query_offset) * query_scale).astype(bf16)
    if direct:
        attended, log_totals, far_keys, far_values, top, mixing, up, down = attend_and_gather(
            queries, keys, values, output_grad * alive, (output_weight, expand_weight, contract_weight)
        )
        top, mixing, down = top.reshape(-1, width), mixing.reshape(-1, width), down.reshape(-1, width)
    else:
        top = to_chip(output_grad * alive)
        far_keys = lax.ppermute(keys, "group", pair)
        far_values = lax.ppermute(values, "group", pair)
        attended, log_totals = attend_forward(queries, keys, far_keys, values, far_values)
    middle = tokens + dot(attended, mixing) + output_bias.astype(f32)
    second_plain, second_inverse = normalize(middle)
    second_rows = (second_plain * gain_two + second_shift.astype(f32)).astype(bf16)
    hidden_pre = dot(second_rows, up) + hidden_offset
    normal_cdf = 0.5 * (1.0 + lax.erf(hidden_pre * root_half))
    hidden = (hidden_pre * normal_cdf).astype(bf16)
    pdf = inv_root_two_pi * jnp.exp(-0.5 * hidden_pre * hidden_pre)
    slope = (normal_cdf + hidden_pre * pdf).astype(bf16)
    output = (middle + dot(hidden, down) + contract_bias.astype(f32)).astype(bf16)

    contract_bias_part = jnp.sum(top.astype(f32), axis=0)
    contract_part = dot(hidden, top, TN).astype(bf16)
    pre_grad = (dot(top, down, NT) * slope).astype(bf16)
    expand_bias_part = jnp.sum(pre_grad.astype(f32), axis=0)
    expand_part = dot(second_rows, pre_grad, TN).astype(bf16)
    second_grad = dot(pre_grad, up, NT)
    second_gain_part = jnp.sum(second_grad * second_plain, axis=0)
    second_shift_part = jnp.sum(second_grad, axis=0)
    middle_grad = top.astype(f32) + normalize_back(second_grad, second_plain, second_inverse, gain_two)
    branch_grad = middle_grad.astype(bf16)
    output_bias_part = jnp.sum(branch_grad.astype(f32), axis=0)
    mixing_part = dot(attended, branch_grad, TN).astype(bf16)
    attended_grad = dot(branch_grad, mixing, NT).astype(bf16)
    if direct:
        query_grad, key_grad, value_grad, output, contract_sum, expand_sum = attend_and_scatter(
            queries, attended_grad, attended, log_totals, keys, far_keys, values, far_values,
            output.reshape(inputs.shape), (contract_part.reshape(4, -1, width), expand_part),
        )
    else:
        output = to_owner(output)
        query_grad, key_own, key_far, value_own, value_far = attend_backward(
            queries, attended_grad, attended, log_totals, keys, far_keys, values, far_values
        )
        key_grad = (key_own.astype(f32) + lax.ppermute(key_far, "group", pair).astype(f32)).astype(bf16)
        value_grad = (value_own.astype(f32) + lax.ppermute(value_far, "group", pair).astype(f32)).astype(
            bf16
        )
    query_bias_part = jnp.sum(query_grad.astype(f32), axis=0)
    value_bias_part = jnp.sum(value_grad.astype(f32), axis=0)
    triple_part = jnp.stack(
        [dot(first_rows, d, TN).astype(bf16) for d in (query_grad, key_grad, value_grad)]
    )
    first_grad = (
        dot(query_grad, triple[0], NT) + dot(key_grad, triple[1], NT) + dot(value_grad, triple[2], NT)
    )
    first_gain_part = jnp.sum(first_grad * first_plain, axis=0)
    first_shift_part = jnp.sum(first_grad, axis=0)
    input_grad = (
        middle_grad + normalize_back(first_grad, first_plain, first_inverse, gain_one)
    ).astype(bf16)

    small_parts = (
        first_gain_part,
        first_shift_part,
        query_bias_part,
        value_bias_part,
        output_bias_part,
        second_gain_part,
        second_shift_part,
        expand_bias_part,
        contract_bias_part,
    )
    if direct:
        mixing_sum, triple_sum, small, input_grad = scatter_last(
            (MIXING, TRIPLE),
            (mixing_part.reshape(4, -1, width), triple_part),
            jnp.concatenate(small_parts).reshape(-1, LANES),
            input_grad.reshape(inputs.shape),
        )
        small, small_sums = small.reshape(-1), []
        for part in small_parts:
            small_sums.append(small[: part.shape[0]])
            small = small[part.shape[0] :]
    else:
        input_grad = to_owner(input_grad)

        def scatter(stacked):
            count = tensor_count * group_count
            part = lax.psum_scatter(stacked.reshape(count, *stacked.shape[2:]), both, scatter_dimension=0)
            return lax.psum(part, "cross").astype(f32)

        depth, across = width // group_count, width // tensor_count
        unit = expand_bias.shape[0]
        triple_sum = scatter(
            triple_part.reshape(3, group_count, depth, tensor_count, across).transpose(3, 1, 0, 2, 4)
        )
        mixing_sum = scatter(
            mixing_part.reshape(tensor_count, across, group_count, depth).transpose(0, 2, 1, 3)
        )
        expand_sum = scatter(
            expand_part.reshape(group_count, depth, tensor_count, unit).transpose(2, 0, 1, 3)
        )
        contract_sum = scatter(
            contract_part.reshape(tensor_count, unit, group_count, depth).transpose(0, 2, 1, 3)
        )
        small_sums = lax.psum(small_parts, ("tensor", "group", "cross"))

    def own_group(full_vector):
        size = full_vector.shape[0] // group_count
        return lax.dynamic_slice_in_dim(full_vector, group_index * size, size)

    def own_split(full_vector):
        size = full_vector.shape[0] // (group_count * tensor_count)
        return lax.dynamic_slice_in_dim(
            full_vector, (tensor_index * group_count + group_index) * size, size
        )

    return (
        output,
        input_grad,
        own_group(small_sums[0]),
        own_group(small_sums[1]),
        triple_sum,
        own_split(small_sums[2]),
        own_split(small_sums[3]),
        mixing_sum,
        own_group(small_sums[4]),
        own_group(small_sums[5]),
        own_group(small_sums[6]),
        expand_sum,
        own_split(small_sums[7]),
        contract_sum,
        own_group(small_sums[8]),
    )


def solution(mesh):
    in_specs = (
        P(("group", "cross"), "tensor", None),
        P(("group", "cross")),
        P(),
        P(),
        P(None, "group", "tensor"),
        P("tensor"),
        P("tensor"),
        P("tensor", "group"),
        P(),
        P(),
        P(),
        P("group", "tensor"),
        P("tensor"),
        P("tensor", "group"),
        P(),
        P(("group", "cross"), "tensor", None),
    )
    out_specs = (
        P(("group", "cross"), "tensor", None),
        P(("group", "cross"), "tensor", None),
        P("group"),
        P("group"),
        P(None, "group", "tensor"),
        P(("tensor", "group")),
        P(("tensor", "group")),
        P("tensor", "group"),
        P("group"),
        P("group"),
        P("group"),
        P("group", "tensor"),
        P(("tensor", "group")),
        P("tensor", "group"),
        P("group"),
    )
    return jax.shard_map(local, mesh=mesh, in_specs=in_specs, out_specs=out_specs, check_vma=False)
```
